32 devices in a mesh: fsdp: 16 (over z, y, core), ctx: 2 (over x).
Axes of the slice: x: 2, y: 2, z: 4, core: 2. Of those that a mesh axis runs over, the one named last changes fastest.
Arguments:
- q_nope: bfloat16 [16, 256, 1024], P('fsdp', 'ctx'), may hold values from -6 to 6
- q_rope: bfloat16 [16, 256, 512], P('fsdp', 'ctx'), may hold values from -450 to 450
- kv_latent: bfloat16 [16, 256, 512], P('fsdp', 'ctx'), may hold values from -6 to 6
- key_rope: bfloat16 [16, 256, 64], P('fsdp', 'ctx'), may hold values from -6 to 6
- weight_codes: bfloat16 [512, 2048], P('fsdp'), may hold values from -0.25 to 0.25
- exponents: int32 [4, 16], replicated, may hold values from -1 to 1
- doc_ids: int32 [16, 256], P('fsdp'), may hold values from 0 to 3, never falling along the last dimension, each value on 1 to 128 neighbouring positions
Outputs:
- scaled_out: bfloat16 [16, 256, 1024], P('fsdp', 'ctx')
The draws below stay inside these ranges and needn't reach their ends.
Inputs may be any that keep to these rules, and one draw needn't show every extreme that they name: `doc_ids`: each document of a sequence covers consecutive positions, at most 128 of them.
All inputs are finite; a program needn't handle non-finite values. Where the reference program divides by a largest or mean magnitude, that divisor is 1e-20 or more.
Results may differ from the reference program's by a relative error of at most 0.0085.
Values may be sent and summed in bfloat16 or wider, within the bound.
A program may use at most 64 MiB of HBM per device.

```python
import math
import jax
import jax.numpy as jnp
import numpy as np
from jax import lax

H = 8
DC = 512
DN = 128
DR = 64
DV = 128
BLK = 128
LEN = 256
SEQS = 16


def rope_pair(key):
    first, second = jax.random.split(jax.random.fold_in(key, 71), 2)
    keys = jnp.clip(jax.random.normal(first, (SEQS, LEN, DR), jnp.float32), -6.0, 6.0)
    queries = jnp.clip(jax.random.normal(second, (SEQS, LEN, H * DR), jnp.float32), -6.0, 6.0)
    return (queries, keys)


def draw_q_rope(key, part):
    return rope_pair(key)[0].astype(jnp.bfloat16)


def draw_key_rope(key, part):
    return rope_pair(key)[1].astype(jnp.bfloat16)


def place_ends(drawn, key, smallest, high):
    shape = drawn.shape
    spot = [jax.random.randint(jax.random.fold_in(key, axis), (), 0, shape[axis]) for axis in range(len(shape))]
    drawn = drawn.at[tuple(spot)].set(smallest)
    longest = shape.index(max(shape))
    spot[longest] = (spot[longest] + 1) % shape[longest]
    return drawn.at[tuple(spot)].set(high)


def level_of(own_key, shape, pieces, low, high):
    def one(dim, shards_of):
        steps = jax.random.uniform(jax.random.fold_in(jax.random.fold_in(own_key, 6), dim), (shards_of,), jnp.float32, low / len(pieces), high / len(pieces))
        return jnp.repeat(jnp.exp(steps), shape[dim] // shards_of).reshape((-1,) + (1,) * (len(shape) - dim - 1))

    factor_of = one(*pieces[0])
    for cut in pieces[1:]:
        factor_of = factor_of * one(*cut)
    return factor_of


def profile(number_of, total, bound, skew):
    loads = [(1 << 20) // math.isqrt(standing ** skew) + 1 for standing in range(2, number_of + 1)]
    spare, given = total - bound - (number_of - 1), [1] * (number_of - 1)
    while spare > 0:
        candidates = [i for i in range(number_of - 1) if given[i] < bound]
        pool, budget = sum([loads[i] for i in candidates]), spare
        for i in candidates:
            addition = min(bound - given[i], max(1, budget * loads[i] // pool), spare)
            given[i] = given[i] + addition
            spare = spare - addition
    return np.array([bound] + given)


def ragged(own_key, number_of, total, limit, lean):
    if number_of == 2:
        one = jax.random.randint(own_key, (), max(1, total - limit), min(limit, total - 1) + 1)
        return jnp.stack([one, total - one])
    tallies = jnp.asarray(profile(number_of, total, limit, lean), jnp.int32)
    pairs = (number_of - 1) // 2
    giver, receiver = tallies[1:1 + 2 * pairs:2], tallies[2:2 + 2 * pairs:2]
    room = jnp.minimum(giver - 1, limit - receiver)
    passed = jax.random.randint(jax.random.fold_in(own_key, 1), (pairs,), 0, 1 << 20) % (room + 1)
    tallies = tallies.at[1:1 + 2 * pairs:2].set(giver - passed).at[2:2 + 2 * pairs:2].set(receiver + passed)
    return tallies[jax.random.permutation(jax.random.fold_in(own_key, 2), number_of)]


def centred(rng, dims, scale, reach, pieces=(), held_as=jnp.bfloat16):
    result = jax.random.normal(rng, dims, jnp.float32) * scale
    if len(pieces) > 0:
        result = level_of(rng, dims, pieces, -0.22, 0.18) * result
    return jnp.clip(result, min=-reach, max=reach).astype(held_as)


def setup_inputs(seed: int = 0) -> dict:
    key_list = jax.random.split(jax.random.key(seed), 8)
    return {
        "q_nope": centred(key_list[0], (SEQS, LEN, H * DN), 1.0, 6.0, ((0, 16), (1, 2))),
        "q_rope": draw_q_rope(jax.random.fold_in(key_list[7], 71), 0),
        "kv_latent": centred(key_list[2], (SEQS, LEN, DC), 1.0, 6.0, ((0, 16), (1, 2))),
        "key_rope": draw_key_rope(jax.random.fold_in(key_list[7], 71), 0),
        "weight_codes": centred(key_list[4], (DC, H * (DN + DV)), DC ** -0.5, 0.25, ((0, 16),)),
        "exponents": place_ends(jax.random.randint(key_list[5], (DC // BLK, H * (DN + DV) // BLK), -1, 2), jax.random.fold_in(key_list[5], 1), -1, 1).astype(jnp.int32),
        "doc_ids": jax.vmap(lambda own: jnp.searchsorted(jnp.cumsum(ragged(own, 4, LEN, LEN // 2, 0)), jnp.arange(LEN), side="right"))(jax.random.split(key_list[6], SEQS)).reshape((SEQS, LEN)).astype(jnp.int32),
    }


def dequantize(codes, exponents):
    nrow, ncol = exponents.shape
    factor = jnp.exp2(exponents.astype(jnp.float32))
    scaled = codes.astype(jnp.float32).reshape(nrow, BLK, ncol, BLK) * factor[:, None, :, None]
    return scaled.reshape(codes.shape).astype(jnp.bfloat16)


def reference(q_nope, q_rope, kv_latent, key_rope, weight_codes, exponents, doc_ids):
    weight = dequantize(weight_codes, exponents)
    width = DN + DV

    def one_sequence(items):
        queries, rotary, latent, rope_keys, docs = items
        keys_values = jnp.dot(latent, weight, preferred_element_type=jnp.float32).astype(jnp.bfloat16)
        keys_values = keys_values.reshape(LEN, H, width)
        k_nope = keys_values[:, :, :DN].astype(jnp.float32)
        values = keys_values[:, :, DN:].astype(jnp.float32)
        queries = queries.reshape(LEN, H, DN).astype(jnp.float32)
        rotary = rotary.reshape(LEN, H, DR).astype(jnp.float32)
        scores = jnp.einsum("qhd,khd->hqk", queries, k_nope)
        scores = scores + jnp.einsum("qhd,kd->hqk", rotary, rope_keys.astype(jnp.float32))
        scores = scores * (DN + DR) ** -0.5
        places = jnp.arange(LEN, dtype=jnp.int32)
        allowed = (places[None, :] <= places[:, None]) & (docs[None, :] == docs[:, None])
        scores = jnp.where(allowed[None], scores, jnp.float32(-1e30))
        top = jnp.max(scores, axis=-1, keepdims=True)
        expo = jnp.exp(scores - top)
        probs = (expo / jnp.sum(expo, axis=-1, keepdims=True)).astype(jnp.bfloat16)
        return jnp.einsum("hqk,khd->qhd", probs.astype(jnp.float32), values)

    attended = lax.map(one_sequence, (q_nope, q_rope, kv_latent, key_rope, doc_ids))
    amax = jnp.max(jnp.abs(attended))
    return (attended / amax).reshape(SEQS, LEN, H * DV).astype(jnp.bfloat16)
```

```python
import functools

import jax
import jax.numpy as jnp
from jax import lax
from jax.experimental import pallas as pl
from jax.experimental.pallas import tpu as pltpu
from jax.sharding import PartitionSpec as P

DN = 128
DR = 64
DV = 128
BLK = 128


def dequantize(codes, exponents):
    nrow, ncol = exponents.shape
    factor = jnp.exp2(exponents.astype(jnp.float32)).astype(jnp.bfloat16)
    scaled = codes.reshape(nrow, BLK, ncol, BLK) * factor[:, None, :, None]
    return scaled.reshape(codes.shape)


def attend(queries, rotary, keys_values, rope_all, query_places, query_docs, docs):
    length = keys_values.shape[0]
    k_nope = keys_values[:, :, :DN]
    values = keys_values[:, :, DN:]
    scores = jnp.einsum("qhd,khd->hqk", queries, k_nope, preferred_element_type=jnp.float32)
    scores = scores + jnp.einsum(
        "qhd,kd->hqk", rotary, rope_all, preferred_element_type=jnp.float32
    )
    scores = scores * (DN + DR) ** (-0.5)
    key_places = jnp.arange(length, dtype=jnp.int32)
    allowed = (key_places[None, :] <= query_places[:, None]) & (
        docs[None, :] == query_docs[:, None]
    )
    scores = jnp.where(allowed[None], scores, jnp.float32(-1e30))
    top = jnp.max(scores, axis=-1, keepdims=True)
    expo = jnp.exp(scores - top)
    probs = (expo / jnp.sum(expo, axis=-1, keepdims=True)).astype(jnp.bfloat16)
    return jnp.einsum("hqk,khd->qhd", probs, values, preferred_element_type=jnp.float32)


def per_device(q_nope, q_rope, kv_latent, key_rope, weight_codes, exponents, doc_ids):
    tok = q_nope.shape[1]
    heads = q_nope.shape[2] // DN
    groups = lax.axis_size("ctx")
    length = tok * groups
    offset = lax.axis_index("ctx") * tok
    docs = doc_ids[0]
    latent_all, rope_all = (
        lax.all_gather(kv_latent[0], "ctx", axis=0, tiled=True),
        lax.all_gather(key_rope[0], "ctx", axis=0, tiled=True),
    )
    codes = lax.all_gather(weight_codes, "fsdp", axis=0, tiled=True)
    weight = dequantize(codes, exponents)
    keys_values = jnp.dot(latent_all, weight, preferred_element_type=jnp.float32).astype(
        jnp.bfloat16
    )
    keys_values = keys_values.reshape(length, heads, DN + DV)
    queries = q_nope[0].reshape(tok, heads, DN)
    rotary = q_rope[0].reshape(tok, heads, DR)
    query_docs = lax.dynamic_slice_in_dim(docs, offset, tok)
    query_places = offset + jnp.arange(tok, dtype=jnp.int32)
    attended = attend(queries, rotary, keys_values, rope_all, query_places, query_docs, docs)
    attended = attended.reshape(tok, heads * DV)
    amax = lax.pmax(jnp.max(jnp.abs(attended)), ("fsdp", "ctx"))
    return (attended / amax).reshape(1, tok, heads * DV).astype(jnp.bfloat16)


MESH = pl.DeviceIdType.MESH
LANES = 128
CHUNKS = 2


def fused_kernel(
    n, groups, qn_hbm, qr_hbm, lat_hbm, rope_hbm, codes_hbm, expo_ref, docs_ref,
    att_ref, amax_ref,
    weight, lat_all, rope_all, qn, qr, peaks,
    z_send, z_recv, y_send, y_recv, x_send, x_recv, c_send, c_recv,
    lat_send, lat_recv, local_sem, own_sem, peak_send, peak_recv, ready,
):
    planes = n // 4
    rows, width = codes_hbm.shape
    tok = qn_hbm.shape[0]
    heads = width // (DN + DV)
    f = lax.axis_index("fsdp")
    x = lax.axis_index("ctx")
    core, row, plane = f % 2, (f // 2) % 2, f // 4

    def at(plane_of, row_of, core_of):
        return (plane_of * 2 + row_of) * 2 + core_of

    to_core = (at(plane, row, 1 - core), x)
    to_row = (at(plane, 1 - row, core), x)
    to_ctx = (f, 1 - x)
    steps = ((1, plane + 1 < planes), (-1, plane >= 1))

    own = pl.ds(pl.multiple_of(x * tok, tok), tok)
    locals_ = [
        pltpu.make_async_copy(lat_hbm, lat_all.at[own], local_sem.at[0]),
        pltpu.make_async_copy(rope_hbm, rope_all.at[own], local_sem.at[1]),
        pltpu.make_async_copy(qn_hbm, qn, local_sem.at[2]),
        pltpu.make_async_copy(qr_hbm, qr, local_sem.at[3]),
        pltpu.make_async_copy(
            codes_hbm, weight.at[pl.ds(pl.multiple_of(f * rows, rows), rows)], own_sem
        ),
    ]
    for copy in locals_:
        copy.start()

    barrier = pltpu.get_barrier_semaphore()
    for target in (to_core, to_row, to_ctx):
        pl.semaphore_signal(barrier, inc=1, device_id=target, device_id_type=MESH)
    count = 3
    for step, there in steps:
        count = count + there.astype(jnp.int32)

        @pl.when(there)
        def _(step=step):
            pl.semaphore_signal(
                barrier, inc=1, device_id=(at(plane + step, row, core), x), device_id_type=MESH
            )

    pl.semaphore_wait(barrier, count)

    cut = width // CHUNKS
    half = cut // 2

    def whole(j):
        return pl.ds(j * cut, cut)

    def part(j, which):
        return pl.ds(pl.multiple_of(j * cut + which * half, LANES), half)

    def piece(plane_of, row_of, core_of, columns):
        start = pl.multiple_of(at(plane_of, row_of, core_of) * rows, rows)
        return weight.at[pl.ds(start, rows), columns]

    def remote(src, dst, send, recv, target):
        return pltpu.make_async_remote_copy(
            src_ref=src, dst_ref=dst, send_sem=send, recv_sem=recv,
            device_id=target, device_id_type=MESH,
        )

    def along(k, d, j, step):
        src = plane - step * k
        dst = piece(src, row, core, whole(j))
        origin = codes_hbm.at[:, whole(j)] if k == 0 else dst
        return remote(
            origin, dst, z_send.at[k, d, j], z_recv.at[k, d, j], (at(plane + step, row, core), x)
        )

    def along_in(k, d, j, step):
        dst = piece(plane - step * k, row, core, whole(j))
        return remote(dst, dst, z_send.at[k - 1, d, j], z_recv.at[k - 1, d, j], to_core)

    def rowwise(k, d, j, step):
        dst = piece(plane - step * k, row, core, part(j, x))
        origin = codes_hbm.at[:, part(j, x)] if k == 0 else dst
        return remote(origin, dst, y_send.at[k, d, j], y_recv.at[k, d, j], to_row)

    def rowwise_in(k, d, j, step):
        dst = piece(plane - step * k, 1 - row, core, part(j, x))
        return remote(dst, dst, y_send.at[k, d, j], y_recv.at[k, d, j], to_row)

    def ctxwise(k, d, j, step):
        dst = piece(plane - step * k, 1 - row, core, part(j, x))
        return remote(dst, dst, x_send.at[k, d, j], x_recv.at[k, d, j], to_ctx)

    def ctxwise_in(k, d, j, step):
        dst = piece(plane - step * k, 1 - row, core, part(j, 1 - x))
        return remote(dst, dst, x_send.at[k, d, j], x_recv.at[k, d, j], to_ctx)

    def corewise(k, d, j, step, which):
        src = plane - step * k
        dst = (
            piece(src, row, core, whole(j))
            if which == 0
            else piece(src, 1 - row, core, part(j, x if which == 1 else 1 - x))
        )
        origin = codes_hbm.at[:, whole(j)] if which == 0 and k == 0 else dst
        return remote(origin, dst, c_send.at[which, k, d, j], c_recv.at[which, k, d, j], to_core)

    def corewise_in(k, d, j, step, which):
        src = plane - step * k
        dst = (
            piece(src, row, 1 - core, whole(j))
            if which == 0
            else piece(src, 1 - row, 1 - core, part(j, x if which == 1 else 1 - x))
        )
        return remote(dst, dst, c_send.at[which, k, d, j], c_recv.at[which, k, d, j], to_core)

    def each(k, body):
        for d, (step, there) in enumerate(steps if k else steps[:1]):
            if k == 0:
                body(d, step)
            else:
                src = plane - step * k
                pl.when((src >= 0) & (src < planes))(functools.partial(body, d, step))

    def z_stage(k, j):
        def body(d, step):
            if k:
                along_in(k, d, j, step).wait_recv()
            for e, (onward, there) in enumerate(steps):
                if k == 0 or e == d:
                    if k < planes - 1:
                        pl.when(there)(along(k, e, j, onward).start)
            rowwise(k, d, j, step).start()
            corewise(k, d, j, step, 0).start()

        each(k, body)

    def y_stage(k, j):
        def body(d, step):
            rowwise_in(k, d, j, step).wait_recv()
            ctxwise(k, d, j, step).start()
            corewise(k, d, j, step, 1).start()

        each(k, body)

    def x_stage(k, j):
        def body(d, step):
            ctxwise_in(k, d, j, step).wait_recv()
            corewise(k, d, j, step, 2).start()

        each(k, body)

    lat_copies = [
        remote(lat_hbm, lat_all.at[own], lat_send.at[0], lat_recv.at[0], to_ctx),
        remote(rope_hbm, rope_all.at[own], lat_send.at[1], lat_recv.at[1], to_ctx),
    ]
    order = [(k, j) for k in range(planes) for j in range(CHUNKS)]
    for t in range(len(order) + 2):
        if t < len(order):
            z_stage(*order[t])
        if t == 0:
            for copy in lat_copies:
                copy.start()
        if 0 <= t - 1 < len(order):
            y_stage(*order[t - 1])
        if 0 <= t - 2:
            x_stage(*order[t - 2])
    for copy in locals_:
        copy.wait()
    for copy in lat_copies:
        copy.wait()
    for k, j in order:
        for which in range(3):
            each(k, lambda d, step: corewise_in(k, d, j, step, which).wait_recv())

    pl.semaphore_signal(ready, inc=1, device_id=to_ctx, device_id_type=MESH)

    length = lat_all.shape[0]
    docs = docs_ref[...].astype(jnp.float32)
    mine = docs_ref[:, own].astype(jnp.float32)
    mine = jnp.broadcast_to(mine, (tok, tok)).T[:, :1]
    places = lax.broadcasted_iota(jnp.int32, (tok, length), 0) + x * tok
    keys_at = lax.broadcasted_iota(jnp.int32, (tok, length), 1)
    allowed = (keys_at <= places) & (jnp.broadcast_to(docs, (tok, length)) == mine)
    latents = lat_all[...]
    rope = rope_all[...]
    blank = jnp.zeros_like(rope)
    rope_of = (
        jnp.concatenate([rope, blank], axis=1), jnp.concatenate([blank, rope], axis=1)
    )
    dims_t = (((1,), (1,)), ((), ()))
    peak = jnp.zeros((tok, DV), jnp.float32)
    for h in range(heads):
        at_col = h * (DN + DV)
        blocks = []
        for b in range(weight.shape[0] // BLK):
            line = []
            for c in range((DN + DV) // BLK):
                power = jnp.full((1, BLK), expo_ref[b, at_col // BLK + c], jnp.int32)
                factor = jnp.exp2(power.astype(jnp.float32)).astype(jnp.bfloat16)
                line.append(
                    weight[b * BLK : (b + 1) * BLK, at_col + c * BLK : at_col + (c + 1) * BLK]
                    * factor
                )
            blocks.append(jnp.concatenate(line, axis=1))
        scaled = jnp.concatenate(blocks, axis=0)
        kv = jnp.dot(latents, scaled, preferred_element_type=jnp.float32).astype(jnp.bfloat16)
        pair = (h // 2) * 2 * DR
        queries = jnp.concatenate(
            [qn[:, h * DN : (h + 1) * DN], qr[:, pair : pair + 2 * DR]], axis=1
        )
        keys = jnp.concatenate([kv[:, :DN], rope_of[h % 2]], axis=1)
        scores = lax.dot_general(queries, keys, dims_t, preferred_element_type=jnp.float32)
        scores = jnp.where(allowed, scores * (DN + DR) ** (-0.5), jnp.float32(-1e30))
        top = jnp.max(scores, axis=-1, keepdims=True)
        expo = jnp.exp(scores - top)
        total = jnp.sum(expo, axis=-1, keepdims=True)
        out = jnp.dot(
            expo.astype(jnp.bfloat16), kv[:, DN:], preferred_element_type=jnp.float32
        ) / total
        att_ref[:, h * DV : (h + 1) * DV] = out
        peak = jnp.maximum(peak, jnp.abs(out))

    me = f * groups + x
    peaks[me] = jnp.max(peak, axis=0, keepdims=True)
    pl.semaphore_wait(ready, 1)
    everyone = n * groups
    for i in range(1, everyone):
        other = lax.rem(me + i, everyone)
        remote(
            peaks.at[me], peaks.at[me], peak_send, peak_recv, (other // groups, other % groups)
        ).start()
    for copy_k, j in order:
        for e, (onward, there) in enumerate(steps):
            if copy_k < planes - 1:
                src = plane - onward * copy_k
                pl.when(there & (src >= 0) & (src < planes))(
                    along(copy_k, e, j, onward).wait_send
                )

        def sent(d, step, k=copy_k, j=j):
            rowwise(k, d, j, step).wait_send()
            ctxwise(k, d, j, step).wait_send()
            for which in range(3):
                corewise(k, d, j, step, which).wait_send()

        each(copy_k, sent)
    others = peaks.at[pl.ds(0, everyone - 1)]
    arrived = remote(others, others, peak_send, peak_recv, to_ctx)
    arrived.wait_send()
    arrived.wait_recv()
    amax_ref[...] = jnp.full(amax_ref.shape, jnp.max(peaks[...]), jnp.float32)


def fused(n, groups, q_nope, q_rope, kv_latent, key_rope, weight_codes, exponents, doc_ids):
    tok = q_nope.shape[1]
    rows, width = weight_codes.shape
    planes = n // 4
    hbm = pl.BlockSpec(memory_space=pl.ANY)
    vmem = pl.BlockSpec(memory_space=pltpu.VMEM)
    dma = pltpu.SemaphoreType.DMA
    links = (planes, 2, CHUNKS)
    attended, amax = pl.pallas_call(
        functools.partial(fused_kernel, n, groups),
        out_shape=(
            jax.ShapeDtypeStruct((tok, width // 2), jnp.float32),
            jax.ShapeDtypeStruct((1, LANES), jnp.float32),
        ),
        in_specs=[hbm] * 5 + [pl.BlockSpec(memory_space=pltpu.SMEM), vmem],
        out_specs=(vmem, vmem),
        scratch_shapes=[
            pltpu.VMEM((rows * n, width), jnp.bfloat16),
            pltpu.VMEM((tok * groups, kv_latent.shape[2]), jnp.bfloat16),
            pltpu.VMEM((tok * groups, key_rope.shape[2]), jnp.bfloat16),
            pltpu.VMEM(q_nope.shape[1:], jnp.bfloat16),
            pltpu.VMEM(q_rope.shape[1:], jnp.bfloat16),
            pltpu.VMEM((n * groups, 1, LANES), jnp.float32),
            dma(links), dma(links), dma(links), dma(links), dma(links), dma(links),
            dma((3, *links)), dma((3, *links)),
            dma((2,)), dma((2,)), dma((4,)), dma, dma, dma,
            pltpu.SemaphoreType.REGULAR,
        ],
        compiler_params=pltpu.CompilerParams(collective_id=0, has_side_effects=True),
    )(q_nope[0], q_rope[0], kv_latent[0], key_rope[0], weight_codes, exponents, doc_ids)
    return (attended / amax[0, 0]).astype(jnp.bfloat16)[None]


def solution(mesh):
    in_specs = (
        P("fsdp", "ctx", None),
        P("fsdp", "ctx", None),
        P("fsdp", "ctx", None),
        P("fsdp", "ctx", None),
        P("fsdp", None),
        P(),
        P("fsdp", None),
    )
    out_specs = P("fsdp", "ctx", None)
    n, groups = mesh.shape["fsdp"], mesh.shape["ctx"]

    def body(*args):
        rows = args[4].shape[0]
        if groups == 2 and n % 4 == 0 and rows % 16 == 0:
            return fused(n, groups, *args)
        return per_device(*args)

    return jax.shard_map(
        body, mesh=mesh, in_specs=in_specs, out_specs=out_specs, check_vma=False
    )
```

```python
import functools

import jax
import jax.numpy as jnp
from jax import lax
from jax.experimental import pallas as pl
from jax.experimental.pallas import tpu as pltpu
from jax.sharding import PartitionSpec as P

DN = 128
DR = 64
DV = 128
BLK = 128


def dequantize(codes, exponents):
    nrow, ncol = exponents.shape
    factor = jnp.exp2(exponents.astype(jnp.float32)).astype(jnp.bfloat16)
    scaled = codes.reshape(nrow, BLK, ncol, BLK) * factor[:, None, :, None]
    return scaled.reshape(codes.shape)


def attend(queries, rotary, keys_values, rope_all, query_places, query_docs, docs):
    length = keys_values.shape[0]
    k_nope = keys_values[:, :, :DN]
    values = keys_values[:, :, DN:]
    scores = jnp.einsum("qhd,khd->hqk", queries, k_nope, preferred_element_type=jnp.float32)
    scores = scores + jnp.einsum(
        "qhd,kd->hqk", rotary, rope_all, preferred_element_type=jnp.float32
    )
    scores = scores * (DN + DR) ** (-0.5)
    key_places = jnp.arange(length, dtype=jnp.int32)
    allowed = (key_places[None, :] <= query_places[:, None]) & (
        docs[None, :] == query_docs[:, None]
    )
    scores = jnp.where(allowed[None], scores, jnp.float32(-1e30))
    top = jnp.max(scores, axis=-1, keepdims=True)
    expo = jnp.exp(scores - top)
    probs = (expo / jnp.sum(expo, axis=-1, keepdims=True)).astype(jnp.bfloat16)
    return jnp.einsum("hqk,khd->qhd", probs, values, preferred_element_type=jnp.float32)


def per_device(q_nope, q_rope, kv_latent, key_rope, weight_codes, exponents, doc_ids):
    tok = q_nope.shape[1]
    heads = q_nope.shape[2] // DN
    groups = lax.axis_size("ctx")
    length = tok * groups
    offset = lax.axis_index("ctx") * tok
    docs = doc_ids[0]
    latent_all, rope_all = (
        lax.all_gather(kv_latent[0], "ctx", axis=0, tiled=True),
        lax.all_gather(key_rope[0], "ctx", axis=0, tiled=True),
    )
    codes = lax.all_gather(weight_codes, "fsdp", axis=0, tiled=True)
    weight = dequantize(codes, exponents)
    keys_values = jnp.dot(latent_all, weight, preferred_element_type=jnp.float32).astype(
        jnp.bfloat16
    )
    keys_values = keys_values.reshape(length, heads, DN + DV)
    queries = q_nope[0].reshape(tok, heads, DN)
    rotary = q_rope[0].reshape(tok, heads, DR)
    query_docs = lax.dynamic_slice_in_dim(docs, offset, tok)
    query_places = offset + jnp.arange(tok, dtype=jnp.int32)
    attended = attend(queries, rotary, keys_values, rope_all, query_places, query_docs, docs)
    attended = attended.reshape(tok, heads * DV)
    amax = lax.pmax(jnp.max(jnp.abs(attended)), ("fsdp", "ctx"))
    return (attended / amax).reshape(1, tok, heads * DV).astype(jnp.bfloat16)


MESH = pl.DeviceIdType.MESH
LANES = 128
RELAYED = 2


def fused_kernel(
    n, groups, qn_hbm, qr_hbm, lat_hbm, rope_hbm, codes_hbm, expo_ref, docs_ref,
    out_ref,
    weight, lat_all, rope_all, qn, qr, attended, bias, peaks,
    z_send, z_recv, y_send, y_recv, x_send, x_recv, c_send, c_recv,
    lat_send, lat_recv, local_sem, own_sem, peak_send, peak_recv, ready, entered,
):
    planes = n // 4
    rows, width = codes_hbm.shape
    hr = rows // 2
    tok = qn_hbm.shape[0]
    heads = width // (DN + DV)
    f = lax.axis_index("fsdp")
    x = lax.axis_index("ctx")
    core, row, plane = f % 2, (f // 2) % 2, f // 4

    def at(plane_of, row_of, core_of):
        return (plane_of * 2 + row_of) * 2 + core_of

    def inside(p):
        return (p >= 0) & (p < planes)

    to_core = (at(plane, row, 1 - core), x)
    to_row = (at(plane, 1 - row, core), x)
    to_ctx = (f, 1 - x)
    steps = (1, -1)

    own = pl.ds(pl.multiple_of(x * tok, tok), tok)
    locals_ = [
        pltpu.make_async_copy(lat_hbm, lat_all.at[own], local_sem.at[0]),
        pltpu.make_async_copy(rope_hbm, rope_all.at[:, own], local_sem.at[1]),
        pltpu.make_async_copy(qn_hbm, qn, local_sem.at[2]),
        pltpu.make_async_copy(qr_hbm, qr, local_sem.at[3]),
        pltpu.make_async_copy(
            codes_hbm, weight.at[pl.ds(pl.multiple_of(f * rows, rows), rows)], own_sem
        ),
    ]

    barrier = pltpu.get_barrier_semaphore()
    for target in (to_core, to_row, to_ctx):
        pl.semaphore_signal(barrier, inc=1, device_id=target, device_id_type=MESH)
    count = 3
    for step in steps:
        there = inside(plane + step)
        count = count + there.astype(jnp.int32)

        @pl.when(there)
        def _(step=step):
            pl.semaphore_signal(
                barrier, inc=1, device_id=(at(plane + step, row, core), x), device_id_type=MESH
            )

    for copy in locals_:
        copy.start()
    pl.semaphore_wait(barrier, count)

    def piece(plane_of, row_of, core_of, which):
        start = pl.multiple_of(at(plane_of, row_of, core_of) * rows + which * hr, hr)
        return weight.at[pl.ds(start, hr)]

    def own_piece(which):
        return codes_hbm.at[pl.ds(pl.multiple_of(which * hr, hr), hr)]

    def remote(src, dst, send, recv, target):
        return pltpu.make_async_remote_copy(
            src_ref=src, dst_ref=dst, send_sem=send, recv_sem=recv,
            device_id=target, device_id_type=MESH,
        )

    def named(c):
        return x if c == 0 else 1 - x

    def z_out(k, d, c):
        step = steps[d]
        source = plane - step if k == RELAYED else plane
        target = plane + step if k <= RELAYED else plane + step * k
        dst = piece(source, row, core, named(c))
        origin = dst if k == RELAYED else own_piece(named(c))
        copy = remote(
            origin, dst, z_send.at[k, d, c], z_recv.at[k, d, c], (at(target, row, core), x)
        )
        return copy, inside(source) & inside(target)

    def z_in(k, d, c):
        dst = piece(plane - steps[d] * k, row, core, named(c))
        return remote(dst, dst, z_send.at[k, d, c], z_recv.at[k, d, c], to_core)

    def y_out(k, d):
        dst = piece(plane - steps[d] * k, row, core, x)
        origin = dst if k else own_piece(x)
        return remote(origin, dst, y_send.at[k, d], y_recv.at[k, d], to_row)

    def y_in(k, d):
        dst = piece(plane - steps[d] * k, 1 - row, core, x)
        return remote(dst, dst, y_send.at[k, d], y_recv.at[k, d], to_row)

    def x_out(k, d):
        dst = piece(plane - steps[d] * k, 1 - row, core, x)
        return remote(dst, dst, x_send.at[k, d], x_recv.at[k, d], to_ctx)

    def x_in(k, d):
        dst = piece(plane - steps[d] * k, 1 - row, core, 1 - x)
        return remote(dst, dst, x_send.at[k, d], x_recv.at[k, d], to_ctx)

    def core_piece(k, d, which, core_of):
        return piece(
            plane - steps[d] * k, row if which < 2 else 1 - row, core_of, named(which % 2)
        )

    def core_out(k, d, which):
        dst = core_piece(k, d, which, core)
        origin = own_piece(named(which)) if which < 2 and k == 0 else dst
        return remote(origin, dst, c_send.at[which, k, d], c_recv.at[which, k, d], to_core)

    def core_in(k, d, which):
        dst = core_piece(k, d, which, 1 - core)
        return remote(dst, dst, c_send.at[which, k, d], c_recv.at[which, k, d], to_core)

    def each(k, body):
        if k == 0:
            body(0)
        elif k < planes:
            for d, step in enumerate(steps):
                pl.when(inside(plane - step * k))(functools.partial(body, d))

    def z_stage(k, c):
        def body(d):
            z_in(k, d, c).wait_recv()
            if k + 1 == RELAYED:
                onward, there = z_out(RELAYED, d, c)
                pl.when(there)(onward.start)
            if c == 0:
                y_out(k, d).start()
            core_out(k, d, c).start()

        each(k, body)

    def y_stage(k):
        def body(d):
            y_in(k, d).wait_recv()
            x_out(k, d).start()
            core_out(k, d, 2).start()

        each(k, body)

    def x_stage(k):
        def body(d):
            x_in(k, d).wait_recv()
            core_out(k, d, 3).start()

        each(k, body)

    lat_copies = [
        remote(lat_hbm, lat_all.at[own], lat_send.at[0], lat_recv.at[0], to_ctx),
        remote(rope_hbm, rope_all.at[:, own], lat_send.at[1], lat_recv.at[1], to_ctx),
    ]
    from_source = [k for k in range(1, planes) if k != RELAYED]

    def send_own(k, c):
        for d in range(2):
            copy, there = z_out(k, d, c)
            pl.when(there)(copy.start)

    y_out(0, 0).start()
    send_own(1, 0)
    for copy in lat_copies:
        copy.start()
    for c in range(2):
        core_out(0, 0, c).start()
    for r in range(1, planes - 1):
        for d, step in enumerate(steps):

            @pl.when(inside(plane + step) & inside(plane - step * r))
            def _(r=r, d=d, step=step):
                pl.semaphore_signal(
                    entered.at[r, d], inc=1,
                    device_id=(at(plane + step, row, core), x), device_id_type=MESH,
                )

        for d, step in enumerate(steps):

            @pl.when(inside(plane - step * (r + 1)))
            def _(r=r, d=d):
                pl.semaphore_wait(entered.at[r, d], 1)

    for k in from_source[1:]:
        send_own(k, 0)
    for k in from_source:
        send_own(k, 1)

    z_stage(1, 0)
    y_stage(0)
    z_stage(1, 1)
    for k in range(2, planes):
        z_stage(k, 0)
    x_stage(0)
    y_stage(1)

    for copy in locals_:
        copy.wait()
    for copy in lat_copies:
        copy.wait()
    length = lat_all.shape[0]
    docs = docs_ref[...].astype(jnp.float32)
    mine = docs_ref[:, own].astype(jnp.float32)
    mine = jnp.broadcast_to(mine, (tok, tok)).T[:, :1]
    places = lax.broadcasted_iota(jnp.int32, (tok, length), 0) + x * tok
    keys_at = lax.broadcasted_iota(jnp.int32, (tok, length), 1)
    allowed = (keys_at <= places) & (jnp.broadcast_to(docs, (tok, length)) == mine)
    bias[...] = jnp.where(allowed, jnp.float32(0), jnp.float32(-1e30))

    for k in range(2, planes):
        y_stage(k)
    x_stage(1)
    for k in range(2, planes):
        z_stage(k, 1)
    for k in range(2, planes):
        x_stage(k)
    for which in range(4):
        for k in range(planes):
            each(k, lambda d: core_in(k, d, which).wait_recv())

    pl.semaphore_signal(ready, inc=1, device_id=to_ctx, device_id_type=MESH)

    latents = lat_all[...]
    rope = rope_all[...]
    blank = jnp.zeros_like(rope)
    rope_of = (
        jnp.concatenate([rope, blank], axis=0).T, jnp.concatenate([blank, rope], axis=0).T
    )
    dims_t = (((1,), (1,)), ((), ()))
    peak = jnp.zeros((tok, DV), jnp.float32)
    for h in range(heads):
        at_col = h * (DN + DV)
        blocks = []
        for b in range(weight.shape[0] // BLK):
            line = []
            for c in range((DN + DV) // BLK):
                power = jnp.full((1, BLK), expo_ref[b, at_col // BLK + c], jnp.int32)
                factor = jnp.exp2(power.astype(jnp.float32)).astype(jnp.bfloat16)
                line.append(
                    weight[b * BLK : (b + 1) * BLK, at_col + c * BLK : at_col + (c + 1) * BLK]
                    * factor
                )
            blocks.append(jnp.concatenate(line, axis=1))
        scaled = jnp.concatenate(blocks, axis=0)
        kv = jnp.dot(latents, scaled, preferred_element_type=jnp.float32).astype(jnp.bfloat16)
        pair = (h // 2) * 2 * DR
        queries = jnp.concatenate(
            [qn[:, h * DN : (h + 1) * DN], qr[:, pair : pair + 2 * DR]], axis=1
        )
        keys = jnp.concatenate([kv[:, :DN], rope_of[h % 2]], axis=1)
        scores = lax.dot_general(queries, keys, dims_t, preferred_element_type=jnp.float32)
        scores = scores * (DN + DR) ** (-0.5) + bias[...]
        top = jnp.max(scores, axis=-1, keepdims=True)
        expo = jnp.exp(scores - top)
        total = jnp.sum(expo, axis=-1, keepdims=True)
        out = jnp.dot(
            expo.astype(jnp.bfloat16), kv[:, DN:], preferred_element_type=jnp.float32
        ) / total
        attended[:, h * DV : (h + 1) * DV] = out
        peak = jnp.maximum(peak, jnp.abs(out))

    me = f * groups + x
    peaks[me] = jnp.max(peak, axis=0, keepdims=True)
    pl.semaphore_wait(ready, 1)
    everyone = n * groups

    def peak_to(target):
        remote(peaks.at[me], peaks.at[me], peak_send, peak_recv, target).start()

    for i in range(planes):
        other = lax.rem(2 * planes - 1 - plane - i, planes)
        for pair in range(7, 0, -1):
            ctx_of = x if pair // 4 == 0 else 1 - x
            row_of = row if pair // 2 % 2 == 0 else 1 - row
            core_of = core if pair % 2 == 0 else 1 - core
            peak_to((at(other, row_of, core_of), ctx_of))
        pl.when(other != plane)(functools.partial(peak_to, (at(other, row, core), x)))
    for c in range(2):
        for k in range(1, planes):
            for d in range(2):
                copy, there = z_out(k, d, c)
                pl.when(there)(copy.wait_send)

    def sent(k, d):
        y_out(k, d).wait_send()
        x_out(k, d).wait_send()
        for which in range(4):
            core_out(k, d, which).wait_send()

    for k in range(planes):
        each(k, functools.partial(sent, k))
    others = peaks.at[pl.ds(0, everyone - 1)]
    arrived = remote(others, others, peak_send, peak_recv, to_ctx)
    arrived.wait_send()
    arrived.wait_recv()
    amax = jnp.max(jnp.max(peaks[...], axis=0), axis=-1, keepdims=True)
    out_ref[...] = (attended[...] / amax).astype(out_ref.dtype)


def fused(n, groups, q_nope, q_rope, kv_latent, key_rope, weight_codes, exponents, doc_ids):
    tok = q_nope.shape[1]
    rows, width = weight_codes.shape
    planes = n // 4
    hbm = pl.BlockSpec(memory_space=pl.ANY)
    vmem = pl.BlockSpec(memory_space=pltpu.VMEM)
    dma = pltpu.SemaphoreType.DMA
    rope = jnp.swapaxes(key_rope, 1, 2)[0]
    scaled_out = pl.pallas_call(
        functools.partial(fused_kernel, n, groups),
        out_shape=jax.ShapeDtypeStruct((tok, width // 2), jnp.bfloat16),
        in_specs=[hbm] * 5 + [pl.BlockSpec(memory_space=pltpu.SMEM), vmem],
        out_specs=vmem,
        scratch_shapes=[
            pltpu.VMEM((rows * n, width), jnp.bfloat16),
            pltpu.VMEM((tok * groups, kv_latent.shape[2]), jnp.bfloat16),
            pltpu.VMEM((rope.shape[0], tok * groups), jnp.bfloat16),
            pltpu.VMEM(q_nope.shape[1:], jnp.bfloat16),
            pltpu.VMEM(q_rope.shape[1:], jnp.bfloat16),
            pltpu.VMEM((tok, width // 2), jnp.float32),
            pltpu.VMEM((tok, tok * groups), jnp.float32),
            pltpu.VMEM((n * groups, 1, LANES), jnp.float32),
            dma((planes, 2, 2)), dma((planes, 2, 2)),
            dma((planes, 2)), dma((planes, 2)), dma((planes, 2)), dma((planes, 2)),
            dma((4, planes, 2)), dma((4, planes, 2)),
            dma((2,)), dma((2,)), dma((4,)), dma, dma, dma,
            pltpu.SemaphoreType.REGULAR, pltpu.SemaphoreType.REGULAR((planes, 2)),
        ],
        compiler_params=pltpu.CompilerParams(collective_id=0, has_side_effects=True),
    )(q_nope[0], q_rope[0], kv_latent[0], rope, weight_codes, exponents, doc_ids)
    return scaled_out[None]


def solution(mesh):
    in_specs = (
        P("fsdp", "ctx", None),
        P("fsdp", "ctx", None),
        P("fsdp", "ctx", None),
        P("fsdp", "ctx", None),
        P("fsdp", None),
        P(),
        P("fsdp", None),
    )
    out_specs = P("fsdp", "ctx", None)
    n, groups = mesh.shape["fsdp"], mesh.shape["ctx"]

    def body(*args):
        rows = args[4].shape[0]
        if groups == 2 and n % 4 == 0 and rows % 32 == 0:
            return fused(n, groups, *args)
        return per_device(*args)

    return jax.shard_map(
        body, mesh=mesh, in_specs=in_specs, out_specs=out_specs, check_vma=False
    )
```

```python
import functools

import jax
import jax.numpy as jnp
from jax import lax
from jax.experimental import pallas as pl
from jax.experimental.pallas import tpu as pltpu
from jax.sharding import PartitionSpec as P

DN = 128
DR = 64
DV = 128
BLK = 128


def dequantize(codes, exponents):
    nrow, ncol = exponents.shape
    factor = jnp.exp2(exponents.astype(jnp.float32)).astype(jnp.bfloat16)
    scaled = codes.reshape(nrow, BLK, ncol, BLK) * factor[:, None, :, None]
    return scaled.reshape(codes.shape)


def attend(queries, rotary, keys_values, rope_all, query_places, query_docs, docs):
    length = keys_values.shape[0]
    k_nope = keys_values[:, :, :DN]
    values = keys_values[:, :, DN:]
    scores = jnp.einsum("qhd,khd->hqk", queries, k_nope, preferred_element_type=jnp.float32)
    scores = scores + jnp.einsum(
        "qhd,kd->hqk", rotary, rope_all, preferred_element_type=jnp.float32
    )
    scores = scores * (DN + DR) ** (-0.5)
    key_places = jnp.arange(length, dtype=jnp.int32)
    allowed = (key_places[None, :] <= query_places[:, None]) & (
        docs[None, :] == query_docs[:, None]
    )
    scores = jnp.where(allowed[None], scores, jnp.float32(-1e30))
    top = jnp.max(scores, axis=-1, keepdims=True)
    expo = jnp.exp(scores - top)
    probs = (expo / jnp.sum(expo, axis=-1, keepdims=True)).astype(jnp.bfloat16)
    return jnp.einsum("hqk,khd->qhd", probs, values, preferred_element_type=jnp.float32)


def per_device(q_nope, q_rope, kv_latent, key_rope, weight_codes, exponents, doc_ids):
    tok = q_nope.shape[1]
    heads = q_nope.shape[2] // DN
    groups = lax.axis_size("ctx")
    length = tok * groups
    offset = lax.axis_index("ctx") * tok
    docs = doc_ids[0]
    latent_all, rope_all = (
        lax.all_gather(kv_latent[0], "ctx", axis=0, tiled=True),
        lax.all_gather(key_rope[0], "ctx", axis=0, tiled=True),
    )
    codes = lax.all_gather(weight_codes, "fsdp", axis=0, tiled=True)
    weight = dequantize(codes, exponents)
    keys_values = jnp.dot(latent_all, weight, preferred_element_type=jnp.float32).astype(
        jnp.bfloat16
    )
    keys_values = keys_values.reshape(length, heads, DN + DV)
    queries = q_nope[0].reshape(tok, heads, DN)
    rotary = q_rope[0].reshape(tok, heads, DR)
    query_docs = lax.dynamic_slice_in_dim(docs, offset, tok)
    query_places = offset + jnp.arange(tok, dtype=jnp.int32)
    attended = attend(queries, rotary, keys_values, rope_all, query_places, query_docs, docs)
    attended = attended.reshape(tok, heads * DV)
    amax = lax.pmax(jnp.max(jnp.abs(attended)), ("fsdp", "ctx"))
    return (attended / amax).reshape(1, tok, heads * DV).astype(jnp.bfloat16)


MESH = pl.DeviceIdType.MESH
LANES = 128
RELAYED = 2


def fused_kernel(
    n, groups, qn_hbm, qr_hbm, lat_hbm, rope_hbm, codes_hbm, expo_ref, docs_ref,
    out_ref,
    weight, lat_all, rope_all, qn, qr, attended, bias, peaks,
    z_send, z_recv, y_send, y_recv, x_send, x_recv, c_send, c_recv,
    lat_send, lat_recv, local_sem, own_sem, peak_send, peak_recv, ready, entered,
):
    planes = n // 4
    rows, width = codes_hbm.shape
    hr = rows // 2
    tok = qn_hbm.shape[0]
    heads = width // (DN + DV)
    f = lax.axis_index("fsdp")
    x = lax.axis_index("ctx")
    core, row, plane = f % 2, (f // 2) % 2, f // 4

    def at(plane_of, row_of, core_of):
        return (plane_of * 2 + row_of) * 2 + core_of

    def inside(p):
        return (p >= 0) & (p < planes)

    to_core = (at(plane, row, 1 - core), x)
    to_row = (at(plane, 1 - row, core), x)
    to_ctx = (f, 1 - x)
    steps = (1, -1)

    own = pl.ds(pl.multiple_of(x * tok, tok), tok)
    locals_ = [
        pltpu.make_async_copy(lat_hbm, lat_all.at[own], local_sem.at[0]),
        pltpu.make_async_copy(rope_hbm, rope_all.at[:, own], local_sem.at[1]),
        pltpu.make_async_copy(qn_hbm, qn, local_sem.at[2]),
        pltpu.make_async_copy(qr_hbm, qr, local_sem.at[3]),
        pltpu.make_async_copy(
            codes_hbm, weight.at[pl.ds(pl.multiple_of(f * rows, rows), rows)], own_sem
        ),
    ]

    barrier = pltpu.get_barrier_semaphore()
    for target in (to_core, to_row, to_ctx):
        pl.semaphore_signal(barrier, inc=1, device_id=target, device_id_type=MESH)
    count = 3
    for step in steps:
        there = inside(plane + step)
        count = count + there.astype(jnp.int32)

        @pl.when(there)
        def _(step=step):
            pl.semaphore_signal(
                barrier, inc=1, device_id=(at(plane + step, row, core), x), device_id_type=MESH
            )

    for copy in locals_:
        copy.start()
    pl.semaphore_wait(barrier, count)

    def piece(plane_of, row_of, core_of, which):
        start = pl.multiple_of(at(plane_of, row_of, core_of) * rows + which * hr, hr)
        return weight.at[pl.ds(start, hr)]

    def own_piece(which):
        return codes_hbm.at[pl.ds(pl.multiple_of(which * hr, hr), hr)]

    def remote(src, dst, send, recv, target):
        return pltpu.make_async_remote_copy(
            src_ref=src, dst_ref=dst, send_sem=send, recv_sem=recv,
            device_id=target, device_id_type=MESH,
        )

    def named(c):
        return x if c == 0 else 1 - x

    def z_out(k, d, c):
        step = steps[d]
        source = plane - step if k == RELAYED else plane
        target = plane + step if k <= RELAYED else plane + step * k
        dst = piece(source, row, core, named(c))
        origin = dst if k == RELAYED else own_piece(named(c))
        copy = remote(
            origin, dst, z_send.at[k, d, c], z_recv.at[k, d, c], (at(target, row, core), x)
        )
        return copy, inside(source) & inside(target)

    def z_in(k, d, c):
        dst = piece(plane - steps[d] * k, row, core, named(c))
        return remote(dst, dst, z_send.at[k, d, c], z_recv.at[k, d, c], to_core)

    def y_out(k, d):
        dst = piece(plane - steps[d] * k, row, core, x)
        origin = dst if k else own_piece(x)
        return remote(origin, dst, y_send.at[k, d], y_recv.at[k, d], to_row)

    def y_in(k, d):
        dst = piece(plane - steps[d] * k, 1 - row, core, x)
        return remote(dst, dst, y_send.at[k, d], y_recv.at[k, d], to_row)

    def x_out(k, d):
        dst = piece(plane - steps[d] * k, 1 - row, core, x)
        return remote(dst, dst, x_send.at[k, d], x_recv.at[k, d], to_ctx)

    def x_in(k, d):
        dst = piece(plane - steps[d] * k, 1 - row, core, 1 - x)
        return remote(dst, dst, x_send.at[k, d], x_recv.at[k, d], to_ctx)

    def core_piece(k, d, which, core_of):
        return piece(
            plane - steps[d] * k, row if which < 2 else 1 - row, core_of, named(which % 2)
        )

    def core_out(k, d, which):
        dst = core_piece(k, d, which, core)
        origin = own_piece(named(which)) if which < 2 and k == 0 else dst
        return remote(origin, dst, c_send.at[which, k, d], c_recv.at[which, k, d], to_core)

    def core_in(k, d, which):
        dst = core_piece(k, d, which, 1 - core)
        return remote(dst, dst, c_send.at[which, k, d], c_recv.at[which, k, d], to_core)

    def each(k, body):
        if k == 0:
            body(0)
        elif k < planes:
            for d, step in enumerate(steps):
                pl.when(inside(plane - step * k))(functools.partial(body, d))

    def z_stage(k, c):
        def body(d):
            z_in(k, d, c).wait_recv()
            if k + 1 == RELAYED:
                onward, there = z_out(RELAYED, d, c)
                pl.when(there)(onward.start)
            if c == 0:
                y_out(k, d).start()
            core_out(k, d, c).start()

        each(k, body)

    def y_stage(k):
        def body(d):
            y_in(k, d).wait_recv()
            x_out(k, d).start()
            core_out(k, d, 2).start()

        each(k, body)

    def x_stage(k):
        def body(d):
            x_in(k, d).wait_recv()
            core_out(k, d, 3).start()

        each(k, body)

    lat_copies = [
        remote(lat_hbm, lat_all.at[own], lat_send.at[0], lat_recv.at[0], to_ctx),
        remote(rope_hbm, rope_all.at[:, own], lat_send.at[1], lat_recv.at[1], to_ctx),
    ]
    from_source = [k for k in range(1, planes) if k != RELAYED]

    def send_own(k, c):
        for d in range(2):
            copy, there = z_out(k, d, c)
            pl.when(there)(copy.start)

    y_out(0, 0).start()
    send_own(1, 0)
    for copy in lat_copies:
        copy.start()
    for c in range(2):
        core_out(0, 0, c).start()
    for r in range(1, planes - 1):
        for d, step in enumerate(steps):

            @pl.when(inside(plane + step) & inside(plane - step * r))
            def _(r=r, d=d, step=step):
                pl.semaphore_signal(
                    entered.at[r, d], inc=1,
                    device_id=(at(plane + step, row, core), x), device_id_type=MESH,
                )

        for d, step in enumerate(steps):

            @pl.when(inside(plane - step * (r + 1)))
            def _(r=r, d=d):
                pl.semaphore_wait(entered.at[r, d], 1)

    for k in from_source[1:]:
        send_own(k, 0)

    z_stage(1, 0)
    for k in from_source:
        send_own(k, 1)
    y_stage(0)
    for k in range(2, planes):
        z_stage(k, 0)
    y_stage(1)
    z_stage(1, 1)
    x_stage(0)

    for copy in locals_:
        copy.wait()
    for copy in lat_copies:
        copy.wait()
    length = lat_all.shape[0]
    docs = docs_ref[...].astype(jnp.float32)
    mine = docs_ref[:, own].astype(jnp.float32)
    mine = jnp.broadcast_to(mine, (tok, tok)).T[:, :1]
    places = lax.broadcasted_iota(jnp.int32, (tok, length), 0) + x * tok
    keys_at = lax.broadcasted_iota(jnp.int32, (tok, length), 1)
    allowed = (keys_at <= places) & (jnp.broadcast_to(docs, (tok, length)) == mine)
    bias[...] = jnp.where(allowed, jnp.float32(0), jnp.float32(-1e30))

    for k in range(2, planes):
        y_stage(k)
    x_stage(1)
    for k in range(2, planes):
        z_stage(k, 1)
    for k in range(2, planes):
        x_stage(k)
    for which in range(4):
        for k in range(planes):
            each(k, lambda d: core_in(k, d, which).wait_recv())

    pl.semaphore_signal(ready, inc=1, device_id=to_ctx, device_id_type=MESH)

    latents = lat_all[...]
    rope = rope_all[...]
    blank = jnp.zeros_like(rope)
    rope_of = (
        jnp.concatenate([rope, blank], axis=0).T, jnp.concatenate([blank, rope], axis=0).T
    )
    dims_t = (((1,), (1,)), ((), ()))
    peak = jnp.zeros((tok, DV), jnp.float32)
    for h in range(heads):
        at_col = h * (DN + DV)
        blocks = []
        for b in range(weight.shape[0] // BLK):
            line = []
            for c in range((DN + DV) // BLK):
                power = jnp.full((1, BLK), expo_ref[b, at_col // BLK + c], jnp.int32)
                factor = jnp.exp2(power.astype(jnp.float32)).astype(jnp.bfloat16)
                line.append(
                    weight[b * BLK : (b + 1) * BLK, at_col + c * BLK : at_col + (c + 1) * BLK]
                    * factor
                )
            blocks.append(jnp.concatenate(line, axis=1))
        scaled = jnp.concatenate(blocks, axis=0)
        kv = jnp.dot(latents, scaled, preferred_element_type=jnp.float32).astype(jnp.bfloat16)
        pair = (h // 2) * 2 * DR
        queries = jnp.concatenate(
            [qn[:, h * DN : (h + 1) * DN], qr[:, pair : pair + 2 * DR]], axis=1
        )
        keys = jnp.concatenate([kv[:, :DN], rope_of[h % 2]], axis=1)
        scores = lax.dot_general(queries, keys, dims_t, preferred_element_type=jnp.float32)
        scores = scores * (DN + DR) ** (-0.5) + bias[...]
        top = jnp.max(scores, axis=-1, keepdims=True)
        expo = jnp.exp(scores - top)
        total = jnp.sum(expo, axis=-1, keepdims=True)
        out = jnp.dot(
            expo.astype(jnp.bfloat16), kv[:, DN:], preferred_element_type=jnp.float32
        ) / total
        attended[:, h * DV : (h + 1) * DV] = out
        peak = jnp.maximum(peak, jnp.abs(out))

    me = f * groups + x
    peaks[me] = jnp.max(peak, axis=0, keepdims=True)
    pl.semaphore_wait(ready, 1)
    everyone = n * groups

    def peak_to(target):
        remote(peaks.at[me], peaks.at[me], peak_send, peak_recv, target).start()

    for i in range(planes):
        other = lax.rem(2 * planes - 1 - plane - i, planes)
        for pair in range(7, 0, -1):
            ctx_of = x if pair // 4 == 0 else 1 - x
            row_of = row if pair // 2 % 2 == 0 else 1 - row
            core_of = core if pair % 2 == 0 else 1 - core
            peak_to((at(other, row_of, core_of), ctx_of))
        pl.when(other != plane)(functools.partial(peak_to, (at(other, row, core), x)))
    for c in range(2):
        for k in range(1, planes):
            for d in range(2):
                copy, there = z_out(k, d, c)
                pl.when(there)(copy.wait_send)

    def sent(k, d):
        y_out(k, d).wait_send()
        x_out(k, d).wait_send()
        for which in range(4):
            core_out(k, d, which).wait_send()

    for k in range(planes):
        each(k, functools.partial(sent, k))
    others = peaks.at[pl.ds(0, everyone - 1)]
    arrived = remote(others, others, peak_send, peak_recv, to_ctx)
    arrived.wait_send()
    arrived.wait_recv()
    amax = jnp.max(jnp.max(peaks[...], axis=0), axis=-1, keepdims=True)
    out_ref[...] = (attended[...] / amax).astype(out_ref.dtype)


def fused(n, groups, q_nope, q_rope, kv_latent, key_rope, weight_codes, exponents, doc_ids):
    tok = q_nope.shape[1]
    rows, width = weight_codes.shape
    planes = n // 4
    hbm = pl.BlockSpec(memory_space=pl.ANY)
    vmem = pl.BlockSpec(memory_space=pltpu.VMEM)
    dma = pltpu.SemaphoreType.DMA
    rope = jnp.swapaxes(key_rope, 1, 2)[0]
    scaled_out = pl.pallas_call(
        functools.partial(fused_kernel, n, groups),
        out_shape=pltpu.VMEM((tok, width // 2), jnp.bfloat16),
        in_specs=[hbm] * 5 + [pl.BlockSpec(memory_space=pltpu.SMEM), vmem],
        out_specs=vmem,
        scratch_shapes=[
            pltpu.VMEM((rows * n, width), jnp.bfloat16),
            pltpu.VMEM((tok * groups, kv_latent.shape[2]), jnp.bfloat16),
            pltpu.VMEM((rope.shape[0], tok * groups), jnp.bfloat16),
            pltpu.VMEM(q_nope.shape[1:], jnp.bfloat16),
            pltpu.VMEM(q_rope.shape[1:], jnp.bfloat16),
            pltpu.VMEM((tok, width // 2), jnp.float32),
            pltpu.VMEM((tok, tok * groups), jnp.float32),
            pltpu.VMEM((n * groups, 1, LANES), jnp.float32),
            dma((planes, 2, 2)), dma((planes, 2, 2)),
            dma((planes, 2)), dma((planes, 2)), dma((planes, 2)), dma((planes, 2)),
            dma((4, planes, 2)), dma((4, planes, 2)),
            dma((2,)), dma((2,)), dma((4,)), dma, dma, dma,
            pltpu.SemaphoreType.REGULAR, pltpu.SemaphoreType.REGULAR((planes, 2)),
        ],
        compiler_params=pltpu.CompilerParams(collective_id=0, has_side_effects=True),
    )(q_nope[0], q_rope[0], kv_latent[0], rope, weight_codes, exponents, doc_ids)
    return scaled_out[None]


def solution(mesh):
    in_specs = (
        P("fsdp", "ctx", None),
        P("fsdp", "ctx", None),
        P("fsdp", "ctx", None),
        P("fsdp", "ctx", None),
        P("fsdp", None),
        P(),
        P("fsdp", None),
    )
    out_specs = P("fsdp", "ctx", None)
    n, groups = mesh.shape["fsdp"], mesh.shape["ctx"]

    def body(*args):
        rows = args[4].shape[0]
        if groups == 2 and n % 4 == 0 and rows % 32 == 0:
            return fused(n, groups, *args)
        return per_device(*args)

    return jax.shard_map(
        body, mesh=mesh, in_specs=in_specs, out_specs=out_specs, check_vma=False
    )
```

```python
import functools

import jax
import jax.numpy as jnp
from jax import lax
from jax.experimental import pallas as pl
from jax.experimental.pallas import tpu as pltpu
from jax.sharding import PartitionSpec as P

DN = 128
DR = 64
DV = 128
BLK = 128


def dequantize(codes, exponents):
    nrow, ncol = exponents.shape
    factor = jnp.exp2(exponents.astype(jnp.float32)).astype(jnp.bfloat16)
    scaled = codes.reshape(nrow, BLK, ncol, BLK) * factor[:, None, :, None]
    return scaled.reshape(codes.shape)


def attend(queries, rotary, keys_values, rope_all, query_places, query_docs, docs):
    length = keys_values.shape[0]
    k_nope = keys_values[:, :, :DN]
    values = keys_values[:, :, DN:]
    scores = jnp.einsum("qhd,khd->hqk", queries, k_nope, preferred_element_type=jnp.float32)
    scores = scores + jnp.einsum(
        "qhd,kd->hqk", rotary, rope_all, preferred_element_type=jnp.float32
    )
    scores = scores * (DN + DR) ** (-0.5)
    key_places = jnp.arange(length, dtype=jnp.int32)
    allowed = (key_places[None, :] <= query_places[:, None]) & (
        docs[None, :] == query_docs[:, None]
    )
    scores = jnp.where(allowed[None], scores, jnp.float32(-1e30))
    top = jnp.max(scores, axis=-1, keepdims=True)
    expo = jnp.exp(scores - top)
    probs = (expo / jnp.sum(expo, axis=-1, keepdims=True)).astype(jnp.bfloat16)
    return jnp.einsum("hqk,khd->qhd", probs, values, preferred_element_type=jnp.float32)


def per_device(q_nope, q_rope, kv_latent, key_rope, weight_codes, exponents, doc_ids):
    tok = q_nope.shape[1]
    heads = q_nope.shape[2] // DN
    groups = lax.axis_size("ctx")
    length = tok * groups
    offset = lax.axis_index("ctx") * tok
    docs = doc_ids[0]
    latent_all, rope_all = (
        lax.all_gather(kv_latent[0], "ctx", axis=0, tiled=True),
        lax.all_gather(key_rope[0], "ctx", axis=0, tiled=True),
    )
    codes = lax.all_gather(weight_codes, "fsdp", axis=0, tiled=True)
    weight = dequantize(codes, exponents)
    keys_values = jnp.dot(latent_all, weight, preferred_element_type=jnp.float32).astype(
        jnp.bfloat16
    )
    keys_values = keys_values.reshape(length, heads, DN + DV)
    queries = q_nope[0].reshape(tok, heads, DN)
    rotary = q_rope[0].reshape(tok, heads, DR)
    query_docs = lax.dynamic_slice_in_dim(docs, offset, tok)
    query_places = offset + jnp.arange(tok, dtype=jnp.int32)
    attended = attend(queries, rotary, keys_values, rope_all, query_places, query_docs, docs)
    attended = attended.reshape(tok, heads * DV)
    amax = lax.pmax(jnp.max(jnp.abs(attended)), ("fsdp", "ctx"))
    return (attended / amax).reshape(1, tok, heads * DV).astype(jnp.bfloat16)


MESH = pl.DeviceIdType.MESH
LANES = 128
RELAYED = 2


def fused_kernel(
    n, groups, qn_hbm, qr_hbm, lat_hbm, rope_hbm, codes_hbm, expo_ref, docs_ref,
    out_ref,
    weight, lat_all, rope_all, qn, qr, attended, bias, partial, peaks,
    z_send, z_recv, y_send, y_recv, x_send, x_recv, c_send, c_recv,
    lat_send, lat_recv, local_sem, own_sem, peak_send, peak_recv, ready, entered,
):
    planes = n // 4
    rows, width = codes_hbm.shape
    hr = rows // 2
    tok = qn_hbm.shape[0]
    heads = width // (DN + DV)
    f = lax.axis_index("fsdp")
    x = lax.axis_index("ctx")
    core, row, plane = f % 2, (f // 2) % 2, f // 4

    def at(plane_of, row_of, core_of):
        return (plane_of * 2 + row_of) * 2 + core_of

    def inside(p):
        return (p >= 0) & (p < planes)

    to_core = (at(plane, row, 1 - core), x)
    to_row = (at(plane, 1 - row, core), x)
    to_ctx = (f, 1 - x)
    steps = (1, -1)

    own = pl.ds(pl.multiple_of(x * tok, tok), tok)
    locals_ = [
        pltpu.make_async_copy(lat_hbm, lat_all.at[own], local_sem.at[0]),
        pltpu.make_async_copy(rope_hbm, rope_all.at[:, own], local_sem.at[1]),
        pltpu.make_async_copy(qn_hbm, qn, local_sem.at[2]),
        pltpu.make_async_copy(qr_hbm, qr, local_sem.at[3]),
        pltpu.make_async_copy(
            codes_hbm, weight.at[pl.ds(pl.multiple_of(f * rows, rows), rows)], own_sem
        ),
    ]

    barrier = pltpu.get_barrier_semaphore()
    for target in (to_core, to_row, to_ctx):
        pl.semaphore_signal(barrier, inc=1, device_id=target, device_id_type=MESH)
    count = 3
    for step in steps:
        there = inside(plane + step)
        count = count + there.astype(jnp.int32)

        @pl.when(there)
        def _(step=step):
            pl.semaphore_signal(
                barrier, inc=1, device_id=(at(plane + step, row, core), x), device_id_type=MESH
            )

    for copy in locals_:
        copy.start()
    pl.semaphore_wait(barrier, count)

    def piece(plane_of, row_of, core_of, which):
        start = pl.multiple_of(at(plane_of, row_of, core_of) * rows + which * hr, hr)
        return weight.at[pl.ds(start, hr)]

    def own_piece(which):
        return codes_hbm.at[pl.ds(pl.multiple_of(which * hr, hr), hr)]

    def remote(src, dst, send, recv, target):
        return pltpu.make_async_remote_copy(
            src_ref=src, dst_ref=dst, send_sem=send, recv_sem=recv,
            device_id=target, device_id_type=MESH,
        )

    def named(c):
        return x if c == 0 else 1 - x

    def z_out(k, d, c):
        step = steps[d]
        source = plane - step if k == RELAYED else plane
        target = plane + step if k <= RELAYED else plane + step * k
        dst = piece(source, row, core, named(c))
        origin = dst if k == RELAYED else own_piece(named(c))
        copy = remote(
            origin, dst, z_send.at[k, d, c], z_recv.at[k, d, c], (at(target, row, core), x)
        )
        return copy, inside(source) & inside(target)

    def z_in(k, d, c):
        dst = piece(plane - steps[d] * k, row, core, named(c))
        return remote(dst, dst, z_send.at[k, d, c], z_recv.at[k, d, c], to_core)

    def y_out(k, d):
        dst = piece(plane - steps[d] * k, row, core, x)
        origin = dst if k else own_piece(x)
        return remote(origin, dst, y_send.at[k, d], y_recv.at[k, d], to_row)

    def y_in(k, d):
        dst = piece(plane - steps[d] * k, 1 - row, core, x)
        return remote(dst, dst, y_send.at[k, d], y_recv.at[k, d], to_row)

    def x_out(k, d):
        dst = piece(plane - steps[d] * k, 1 - row, core, x)
        return remote(dst, dst, x_send.at[k, d], x_recv.at[k, d], to_ctx)

    def x_in(k, d):
        dst = piece(plane - steps[d] * k, 1 - row, core, 1 - x)
        return remote(dst, dst, x_send.at[k, d], x_recv.at[k, d], to_ctx)

    def core_piece(k, d, which, core_of):
        return piece(
            plane - steps[d] * k, row if which < 2 else 1 - row, core_of, named(which % 2)
        )

    def core_out(k, d, which):
        dst = core_piece(k, d, which, core)
        origin = own_piece(named(which)) if which < 2 and k == 0 else dst
        return remote(origin, dst, c_send.at[which, k, d], c_recv.at[which, k, d], to_core)

    def core_in(k, d, which):
        dst = core_piece(k, d, which, 1 - core)
        return remote(dst, dst, c_send.at[which, k, d], c_recv.at[which, k, d], to_core)

    def each(k, body):
        if k == 0:
            body(0)
        elif k < planes:
            for d, step in enumerate(steps):
                pl.when(inside(plane - step * k))(functools.partial(body, d))

    def z_stage(k, c):
        def body(d):
            z_in(k, d, c).wait_recv()
            if k + 1 == RELAYED:
                onward, there = z_out(RELAYED, d, c)
                pl.when(there)(onward.start)
            if c == 0:
                y_out(k, d).start()
            core_out(k, d, c).start()

        each(k, body)

    def y_stage(k):
        def body(d):
            y_in(k, d).wait_recv()
            x_out(k, d).start()
            core_out(k, d, 2).start()

        each(k, body)

    def x_stage(k):
        def body(d):
            x_in(k, d).wait_recv()
            core_out(k, d, 3).start()

        each(k, body)

    lat_copies = [
        remote(lat_hbm, lat_all.at[own], lat_send.at[0], lat_recv.at[0], to_ctx),
        remote(rope_hbm, rope_all.at[:, own], lat_send.at[1], lat_recv.at[1], to_ctx),
    ]
    from_source = [k for k in range(1, planes) if k != RELAYED]

    def send_own(k, c):
        for d in range(2):
            copy, there = z_out(k, d, c)
            pl.when(there)(copy.start)

    y_out(0, 0).start()
    send_own(1, 0)
    for copy in lat_copies:
        copy.start()
    for c in range(2):
        core_out(0, 0, c).start()
    for r in range(1, planes - 1):
        for d, step in enumerate(steps):

            @pl.when(inside(plane + step) & inside(plane - step * r))
            def _(r=r, d=d, step=step):
                pl.semaphore_signal(
                    entered.at[r, d], inc=1,
                    device_id=(at(plane + step, row, core), x), device_id_type=MESH,
                )

        for d, step in enumerate(steps):

            @pl.when(inside(plane - step * (r + 1)))
            def _(r=r, d=d):
                pl.semaphore_wait(entered.at[r, d], 1)

    for k in from_source[1:]:
        send_own(k, 0)

    z_stage(1, 0)
    y_stage(0)
    send_own(1, 1)
    z_stage(2, 0)
    for k in from_source[1:]:
        send_own(k, 1)
    for k in range(3, planes):
        z_stage(k, 0)
    y_stage(1)
    z_stage(1, 1)
    x_stage(0)

    for copy in locals_:
        copy.wait()
    for copy in lat_copies:
        copy.wait()
    length = lat_all.shape[0]
    docs = docs_ref[...].astype(jnp.float32)
    mine = docs_ref[:, own].astype(jnp.float32)
    mine = jnp.broadcast_to(mine, (tok, tok)).T[:, :1]
    places = lax.broadcasted_iota(jnp.int32, (tok, length), 0) + x * tok
    keys_at = lax.broadcasted_iota(jnp.int32, (tok, length), 1)
    allowed = (keys_at <= places) & (jnp.broadcast_to(docs, (tok, length)) == mine)
    bias[...] = jnp.where(allowed, jnp.float32(0), jnp.float32(-1e30))

    wide = DN + DV
    last = jnp.where(plane < planes // 2, planes - 1, 0)

    def product(source, h):
        block = pl.ds(pl.multiple_of(source * BLK, BLK), BLK)
        line = []
        for c in range(wide // BLK):
            power = jnp.full((1, BLK), expo_ref[source, h * wide // BLK + c], jnp.int32)
            factor = jnp.exp2(power.astype(jnp.float32)).astype(jnp.bfloat16)
            line.append(
                weight[block, h * wide + c * BLK : h * wide + (c + 1) * BLK] * factor
            )
        return jnp.dot(
            lat_all[:, block], jnp.concatenate(line, axis=1), preferred_element_type=jnp.float32
        )

    def add_plane(k):
        def body(d):
            source = plane - steps[d] * k
            for which in range(4):
                core_in(k, d, which).wait_recv()

            def add():
                for h in range(heads):
                    columns = slice(h * wide, (h + 1) * wide)
                    if k == 0:
                        partial[:, columns] = product(source, h)
                    else:
                        partial[:, columns] += product(source, h)

            if k == 0:
                add()
            else:
                pl.when(source != last)(add)

        each(k, body)

    y_stage(2)
    add_plane(0)
    for k in range(3, planes):
        y_stage(k)
    x_stage(1)
    for k in range(2, planes):
        z_stage(k, 1)
    x_stage(2)
    add_plane(1)
    for k in range(3, planes):
        x_stage(k)
    for k in range(2, planes):
        add_plane(k)

    pl.semaphore_signal(ready, inc=1, device_id=to_ctx, device_id_type=MESH)

    rope = rope_all[...]
    blank = jnp.zeros_like(rope)
    rope_of = (
        jnp.concatenate([rope, blank], axis=0).T, jnp.concatenate([blank, rope], axis=0).T
    )
    dims_t = (((1,), (1,)), ((), ()))
    peak = jnp.zeros((tok, DV), jnp.float32)
    for h in range(heads):
        columns = slice(h * wide, (h + 1) * wide)
        kv = (partial[:, columns] + product(last, h)).astype(jnp.bfloat16)
        pair = (h // 2) * 2 * DR
        queries = jnp.concatenate(
            [qn[:, h * DN : (h + 1) * DN], qr[:, pair : pair + 2 * DR]], axis=1
        )
        keys = jnp.concatenate([kv[:, :DN], rope_of[h % 2]], axis=1)
        scores = lax.dot_general(queries, keys, dims_t, preferred_element_type=jnp.float32)
        scores = scores * (DN + DR) ** (-0.5) + bias[...]
        top = jnp.max(scores, axis=-1, keepdims=True)
        expo = jnp.exp(scores - top)
        total = jnp.sum(expo, axis=-1, keepdims=True)
        out = jnp.dot(
            expo.astype(jnp.bfloat16), kv[:, DN:], preferred_element_type=jnp.float32
        ) / total
        attended[:, h * DV : (h + 1) * DV] = out
        peak = jnp.maximum(peak, jnp.abs(out))

    me = f * groups + x
    peaks[me] = jnp.max(peak, axis=0, keepdims=True)
    pl.semaphore_wait(ready, 1)
    everyone = n * groups

    def peak_to(target):
        remote(peaks.at[me], peaks.at[me], peak_send, peak_recv, target).start()

    for i in range(planes):
        other = lax.rem(2 * planes - 1 - plane - i, planes)
        for pair in range(7, 0, -1):
            ctx_of = x if pair // 4 == 0 else 1 - x
            row_of = row if pair // 2 % 2 == 0 else 1 - row
            core_of = core if pair % 2 == 0 else 1 - core
            peak_to((at(other, row_of, core_of), ctx_of))
        pl.when(other != plane)(functools.partial(peak_to, (at(other, row, core), x)))
    for c in range(2):
        for k in range(1, planes):
            for d in range(2):
                copy, there = z_out(k, d, c)
                pl.when(there)(copy.wait_send)

    def sent(k, d):
        y_out(k, d).wait_send()
        x_out(k, d).wait_send()
        for which in range(4):
            core_out(k, d, which).wait_send()

    for k in range(planes):
        each(k, functools.partial(sent, k))
    others = peaks.at[pl.ds(0, everyone - 1)]
    arrived = remote(others, others, peak_send, peak_recv, to_ctx)
    arrived.wait_send()
    arrived.wait_recv()
    amax = jnp.max(jnp.max(peaks[...], axis=0), axis=-1, keepdims=True)
    out_ref[...] = (attended[...] / amax).astype(out_ref.dtype)


def fused(n, groups, q_nope, q_rope, kv_latent, key_rope, weight_codes, exponents, doc_ids):
    tok = q_nope.shape[1]
    rows, width = weight_codes.shape
    planes = n // 4
    hbm = pl.BlockSpec(memory_space=pl.ANY)
    vmem = pl.BlockSpec(memory_space=pltpu.VMEM)
    dma = pltpu.SemaphoreType.DMA
    rope = jnp.swapaxes(key_rope, 1, 2)[0]
    scaled_out = pl.pallas_call(
        functools.partial(fused_kernel, n, groups),
        out_shape=pltpu.VMEM((tok, width // 2), jnp.bfloat16),
        in_specs=[hbm] * 5 + [pl.BlockSpec(memory_space=pltpu.SMEM), vmem],
        out_specs=vmem,
        scratch_shapes=[
            pltpu.VMEM((rows * n, width), jnp.bfloat16),
            pltpu.VMEM((tok * groups, kv_latent.shape[2]), jnp.bfloat16),
            pltpu.VMEM((rope.shape[0], tok * groups), jnp.bfloat16),
            pltpu.VMEM(q_nope.shape[1:], jnp.bfloat16),
            pltpu.VMEM(q_rope.shape[1:], jnp.bfloat16),
            pltpu.VMEM((tok, width // 2), jnp.float32),
            pltpu.VMEM((tok, tok * groups), jnp.float32),
            pltpu.VMEM((tok * groups, width), jnp.float32),
            pltpu.VMEM((n * groups, 1, LANES), jnp.float32),
            dma((planes, 2, 2)), dma((planes, 2, 2)),
            dma((planes, 2)), dma((planes, 2)), dma((planes, 2)), dma((planes, 2)),
            dma((4, planes, 2)), dma((4, planes, 2)),
            dma((2,)), dma((2,)), dma((4,)), dma, dma, dma,
            pltpu.SemaphoreType.REGULAR, pltpu.SemaphoreType.REGULAR((planes, 2)),
        ],
        compiler_params=pltpu.CompilerParams(collective_id=0, has_side_effects=True),
    )(q_nope[0], q_rope[0], kv_latent[0], rope, weight_codes, exponents, doc_ids)
    return scaled_out[None]


def solution(mesh):
    in_specs = (
        P("fsdp", "ctx", None),
        P("fsdp", "ctx", None),
        P("fsdp", "ctx", None),
        P("fsdp", "ctx", None),
        P("fsdp", None),
        P(),
        P("fsdp", None),
    )
    out_specs = P("fsdp", "ctx", None)
    n, groups = mesh.shape["fsdp"], mesh.shape["ctx"]

    def body(*args):
        rows = args[4].shape[0]
        if groups == 2 and n % 4 == 0 and rows % 32 == 0 and rows * 4 == BLK and n >= 8:
            return fused(n, groups, *args)
        return per_device(*args)

    return jax.shard_map(
        body, mesh=mesh, in_specs=in_specs, out_specs=out_specs, check_vma=False
    )
```

```python
import functools

import jax
import jax.numpy as jnp
from jax import lax
from jax.experimental import pallas as pl
from jax.experimental.pallas import tpu as pltpu
from jax.sharding import PartitionSpec as P

DN = 128
DR = 64
DV = 128
BLK = 128


def dequantize(codes, exponents):
    nrow, ncol = exponents.shape
    factor = jnp.exp2(exponents.astype(jnp.float32)).astype(jnp.bfloat16)
    scaled = codes.reshape(nrow, BLK, ncol, BLK) * factor[:, None, :, None]
    return scaled.reshape(codes.shape)


def attend(queries, rotary, keys_values, rope_all, query_places, query_docs, docs):
    length = keys_values.shape[0]
    k_nope = keys_values[:, :, :DN]
    values = keys_values[:, :, DN:]
    scores = jnp.einsum("qhd,khd->hqk", queries, k_nope, preferred_element_type=jnp.float32)
    scores = scores + jnp.einsum(
        "qhd,kd->hqk", rotary, rope_all, preferred_element_type=jnp.float32
    )
    scores = scores * (DN + DR) ** (-0.5)
    key_places = jnp.arange(length, dtype=jnp.int32)
    allowed = (key_places[None, :] <= query_places[:, None]) & (
        docs[None, :] == query_docs[:, None]
    )
    scores = jnp.where(allowed[None], scores, jnp.float32(-1e30))
    top = jnp.max(scores, axis=-1, keepdims=True)
    expo = jnp.exp(scores - top)
    probs = (expo / jnp.sum(expo, axis=-1, keepdims=True)).astype(jnp.bfloat16)
    return jnp.einsum("hqk,khd->qhd", probs, values, preferred_element_type=jnp.float32)


def per_device(q_nope, q_rope, kv_latent, key_rope, weight_codes, exponents, doc_ids):
    tok = q_nope.shape[1]
    heads = q_nope.shape[2] // DN
    groups = lax.axis_size("ctx")
    length = tok * groups
    offset = lax.axis_index("ctx") * tok
    docs = doc_ids[0]
    latent_all, rope_all = (
        lax.all_gather(kv_latent[0], "ctx", axis=0, tiled=True),
        lax.all_gather(key_rope[0], "ctx", axis=0, tiled=True),
    )
    codes = lax.all_gather(weight_codes, "fsdp", axis=0, tiled=True)
    weight = dequantize(codes, exponents)
    keys_values = jnp.dot(latent_all, weight, preferred_element_type=jnp.float32).astype(
        jnp.bfloat16
    )
    keys_values = keys_values.reshape(length, heads, DN + DV)
    queries = q_nope[0].reshape(tok, heads, DN)
    rotary = q_rope[0].reshape(tok, heads, DR)
    query_docs = lax.dynamic_slice_in_dim(docs, offset, tok)
    query_places = offset + jnp.arange(tok, dtype=jnp.int32)
    attended = attend(queries, rotary, keys_values, rope_all, query_places, query_docs, docs)
    attended = attended.reshape(tok, heads * DV)
    amax = lax.pmax(jnp.max(jnp.abs(attended)), ("fsdp", "ctx"))
    return (attended / amax).reshape(1, tok, heads * DV).astype(jnp.bfloat16)


MESH = pl.DeviceIdType.MESH
LANES = 128
RELAYED = 2


def fused_kernel(
    n, groups, qn_hbm, qr_hbm, lat_hbm, rope_hbm, codes_hbm, expo_hbm, docs_hbm,
    out_ref,
    weight, lat_all, rope_all, qn, qr, attended, bias, partial, rope_of, peaks, expo_ref, docs_ref,
    z_send, z_recv, y_send, y_recv, x_send, x_recv, c_send, c_recv,
    lat_send, lat_recv, local_sem, own_sem, peak_send, peak_recv, ready, entered,
):
    planes = n // 4
    rows, width = codes_hbm.shape
    hr = rows // 2
    tok = qn_hbm.shape[0]
    heads = width // (DN + DV)
    f = lax.axis_index("fsdp")
    x = lax.axis_index("ctx")
    core, row, plane = f % 2, (f // 2) % 2, f // 4

    def at(plane_of, row_of, core_of):
        return (plane_of * 2 + row_of) * 2 + core_of

    def inside(p):
        return (p >= 0) & (p < planes)

    to_core = (at(plane, row, 1 - core), x)
    to_row = (at(plane, 1 - row, core), x)
    to_ctx = (f, 1 - x)
    steps = (1, -1)

    own = pl.ds(pl.multiple_of(x * tok, tok), tok)
    locals_ = [
        pltpu.make_async_copy(lat_hbm, lat_all.at[own], local_sem.at[0]),
        pltpu.make_async_copy(rope_hbm, rope_all.at[:, own], local_sem.at[1]),
        pltpu.make_async_copy(qn_hbm, qn, local_sem.at[2]),
        pltpu.make_async_copy(qr_hbm, qr, local_sem.at[3]),
        pltpu.make_async_copy(expo_hbm, expo_ref, local_sem.at[4]),
        pltpu.make_async_copy(docs_hbm, docs_ref, local_sem.at[5]),
        pltpu.make_async_copy(
            codes_hbm, weight.at[pl.ds(pl.multiple_of(f * rows, rows), rows)], own_sem
        ),
    ]

    barrier = pltpu.get_barrier_semaphore()
    for target in (to_core, to_row, to_ctx):
        pl.semaphore_signal(barrier, inc=1, device_id=target, device_id_type=MESH)
    count = 3
    for step in steps:
        there = inside(plane + step)
        count = count + there.astype(jnp.int32)

        @pl.when(there)
        def _(step=step):
            pl.semaphore_signal(
                barrier, inc=1, device_id=(at(plane + step, row, core), x), device_id_type=MESH
            )

    for copy in locals_:
        copy.start()
    pl.semaphore_wait(barrier, count)

    def piece(plane_of, row_of, core_of, which):
        start = pl.multiple_of(at(plane_of, row_of, core_of) * rows + which * hr, hr)
        return weight.at[pl.ds(start, hr)]

    def own_piece(which):
        return codes_hbm.at[pl.ds(pl.multiple_of(which * hr, hr), hr)]

    def remote(src, dst, send, recv, target):
        return pltpu.make_async_remote_copy(
            src_ref=src, dst_ref=dst, send_sem=send, recv_sem=recv,
            device_id=target, device_id_type=MESH,
        )

    def named(c):
        return x if c == 0 else 1 - x

    def z_out(k, d, c):
        step = steps[d]
        source = plane - step if k == RELAYED else plane
        target = plane + step if k <= RELAYED else plane + step * k
        dst = piece(source, row, core, named(c))
        origin = dst if k == RELAYED else own_piece(named(c))
        copy = remote(
            origin, dst, z_send.at[k, d, c], z_recv.at[k, d, c], (at(target, row, core), x)
        )
        return copy, inside(source) & inside(target)

    def z_in(k, d, c):
        dst = piece(plane - steps[d] * k, row, core, named(c))
        return remote(dst, dst, z_send.at[k, d, c], z_recv.at[k, d, c], to_core)

    def y_out(k, d):
        dst = piece(plane - steps[d] * k, row, core, x)
        origin = dst if k else own_piece(x)
        return remote(origin, dst, y_send.at[k, d], y_recv.at[k, d], to_row)

    def y_in(k, d):
        dst = piece(plane - steps[d] * k, 1 - row, core, x)
        return remote(dst, dst, y_send.at[k, d], y_recv.at[k, d], to_row)

    def x_out(k, d):
        dst = piece(plane - steps[d] * k, 1 - row, core, x)
        return remote(dst, dst, x_send.at[k, d], x_recv.at[k, d], to_ctx)

    def x_in(k, d):
        dst = piece(plane - steps[d] * k, 1 - row, core, 1 - x)
        return remote(dst, dst, x_send.at[k, d], x_recv.at[k, d], to_ctx)

    def core_piece(k, d, which, core_of):
        return piece(
            plane - steps[d] * k, row if which < 2 else 1 - row, core_of, named(which % 2)
        )

    def core_out(k, d, which):
        dst = core_piece(k, d, which, core)
        origin = own_piece(named(which)) if which < 2 and k == 0 else dst
        return remote(origin, dst, c_send.at[which, k, d], c_recv.at[which, k, d], to_core)

    def core_in(k, d, which):
        dst = core_piece(k, d, which, 1 - core)
        return remote(dst, dst, c_send.at[which, k, d], c_recv.at[which, k, d], to_core)

    def each(k, body):
        if k == 0:
            body(0)
        elif k < planes:
            for d, step in enumerate(steps):
                pl.when(inside(plane - step * k))(functools.partial(body, d))

    def z_stage(k, c):
        def body(d):
            z_in(k, d, c).wait_recv()
            if k + 1 == RELAYED:
                onward, there = z_out(RELAYED, d, c)
                pl.when(there)(onward.start)
            if c == 0:
                y_out(k, d).start()
            core_out(k, d, c).start()

        each(k, body)

    def y_stage(k):
        def body(d):
            y_in(k, d).wait_recv()
            x_out(k, d).start()
            core_out(k, d, 2).start()

        each(k, body)

    def x_stage(k):
        def body(d):
            x_in(k, d).wait_recv()
            core_out(k, d, 3).start()

        each(k, body)

    lat_copies = [
        remote(lat_hbm, lat_all.at[own], lat_send.at[0], lat_recv.at[0], to_ctx),
        remote(rope_hbm, rope_all.at[:, own], lat_send.at[1], lat_recv.at[1], to_ctx),
    ]
    from_source = [k for k in range(1, planes) if k != RELAYED]

    def send_own(k, c):
        for d in range(2):
            copy, there = z_out(k, d, c)
            pl.when(there)(copy.start)

    y_out(0, 0).start()
    send_own(1, 0)
    for copy in lat_copies:
        copy.start()
    for c in range(2):
        core_out(0, 0, c).start()
    for r in range(1, planes - 1):
        for d, step in enumerate(steps):

            @pl.when(inside(plane + step) & inside(plane - step * r))
            def _(r=r, d=d, step=step):
                pl.semaphore_signal(
                    entered.at[r, d], inc=1,
                    device_id=(at(plane + step, row, core), x), device_id_type=MESH,
                )

        for d, step in enumerate(steps):

            @pl.when(inside(plane - step * (r + 1)))
            def _(r=r, d=d):
                pl.semaphore_wait(entered.at[r, d], 1)

    for k in from_source[1:]:
        send_own(k, 0)

    z_stage(1, 0)
    y_stage(0)
    send_own(1, 1)
    z_stage(2, 0)
    for k in from_source[1:]:
        send_own(k, 1)
    z_stage(1, 1)
    y_stage(1)
    for k in range(3, planes):
        z_stage(k, 0)
    x_stage(0)

    for copy in locals_:
        copy.wait()
    for copy in lat_copies:
        copy.wait()
    length = lat_all.shape[0]
    docs = docs_ref[...].astype(jnp.float32)
    mine = docs_ref[:, own].astype(jnp.float32)
    mine = jnp.broadcast_to(mine, (tok, tok)).T[:, :1]
    places = lax.broadcasted_iota(jnp.int32, (tok, length), 0) + x * tok
    keys_at = lax.broadcasted_iota(jnp.int32, (tok, length), 1)
    allowed = (keys_at <= places) & (jnp.broadcast_to(docs, (tok, length)) == mine)
    bias[...] = jnp.where(allowed, jnp.float32(0), jnp.float32(-1e30))
    rope = rope_all[...]
    blank = jnp.zeros_like(rope)
    rope_of[0] = jnp.concatenate([rope, blank], axis=0).T
    rope_of[1] = jnp.concatenate([blank, rope], axis=0).T

    wide = DN + DV
    last = jnp.where(plane < planes // 2, planes - 1, 0)

    def product(source, h):
        block = pl.ds(pl.multiple_of(source * BLK, BLK), BLK)
        line = []
        for c in range(wide // BLK):
            power = jnp.full((1, BLK), expo_ref[source, h * wide // BLK + c], jnp.int32)
            factor = jnp.exp2(power.astype(jnp.float32)).astype(jnp.bfloat16)
            line.append(
                weight[block, h * wide + c * BLK : h * wide + (c + 1) * BLK] * factor
            )
        return jnp.dot(
            lat_all[:, block], jnp.concatenate(line, axis=1), preferred_element_type=jnp.float32
        )

    def add_plane(k):
        def body(d):
            source = plane - steps[d] * k
            for which in range(4):
                core_in(k, d, which).wait_recv()

            def add():
                for h in range(heads):
                    columns = slice(h * wide, (h + 1) * wide)
                    if k == 0:
                        partial[:, columns] = product(source, h)
                    else:
                        partial[:, columns] += product(source, h)

            if k == 0:
                add()
            else:
                pl.when(source != last)(add)

        each(k, body)

    y_stage(2)
    add_plane(0)
    for k in range(3, planes):
        y_stage(k)
    x_stage(1)
    for k in range(2, planes):
        z_stage(k, 1)
    x_stage(2)
    add_plane(1)
    for k in range(3, planes):
        x_stage(k)
    for k in range(2, planes):
        add_plane(k)

    pl.semaphore_signal(ready, inc=1, device_id=to_ctx, device_id_type=MESH)

    dims_t = (((1,), (1,)), ((), ()))
    peak = jnp.zeros((tok, DV), jnp.float32)
    for h in range(heads):
        columns = slice(h * wide, (h + 1) * wide)
        kv = (partial[:, columns] + product(last, h)).astype(jnp.bfloat16)
        pair = (h // 2) * 2 * DR
        queries = jnp.concatenate(
            [qn[:, h * DN : (h + 1) * DN], qr[:, pair : pair + 2 * DR]], axis=1
        )
        keys = jnp.concatenate([kv[:, :DN], rope_of[h % 2]], axis=1)
        scores = lax.dot_general(queries, keys, dims_t, preferred_element_type=jnp.float32)
        scores = scores * (DN + DR) ** (-0.5) + bias[...]
        top = jnp.max(scores, axis=-1, keepdims=True)
        expo = jnp.exp(scores - top)
        total = jnp.sum(expo, axis=-1, keepdims=True)
        out = jnp.dot(
            expo.astype(jnp.bfloat16), kv[:, DN:], preferred_element_type=jnp.float32
        ) / total
        attended[:, h * DV : (h + 1) * DV] = out
        peak = jnp.maximum(peak, jnp.abs(out))

    me = f * groups + x
    peaks[me] = jnp.max(peak, axis=0, keepdims=True)
    pl.semaphore_wait(ready, 1)
    everyone = n * groups

    def peak_to(target):
        remote(peaks.at[me], peaks.at[me], peak_send, peak_recv, target).start()

    for i in range(planes):
        other = lax.rem(2 * planes - 1 - plane - i, planes)
        for pair in range(7, 0, -1):
            ctx_of = x if pair // 4 == 0 else 1 - x
            row_of = row if pair // 2 % 2 == 0 else 1 - row
            core_of = core if pair % 2 == 0 else 1 - core
            peak_to((at(other, row_of, core_of), ctx_of))
        pl.when(other != plane)(functools.partial(peak_to, (at(other, row, core), x)))
    for c in range(2):
        for k in range(1, planes):
            for d in range(2):
                copy, there = z_out(k, d, c)
                pl.when(there)(copy.wait_send)

    def sent(k, d):
        y_out(k, d).wait_send()
        x_out(k, d).wait_send()
        for which in range(4):
            core_out(k, d, which).wait_send()

    for k in range(planes):
        each(k, functools.partial(sent, k))
    others = peaks.at[pl.ds(0, everyone - 1)]
    arrived = remote(others, others, peak_send, peak_recv, to_ctx)
    arrived.wait_send()
    arrived.wait_recv()
    amax = jnp.max(jnp.max(peaks[...], axis=0), axis=-1, keepdims=True)
    out_ref[...] = (attended[...] / amax).astype(out_ref.dtype)


def fused(n, groups, q_nope, q_rope, kv_latent, key_rope, weight_codes, exponents, doc_ids):
    tok = q_nope.shape[1]
    rows, width = weight_codes.shape
    planes = n // 4
    hbm = pl.BlockSpec(memory_space=pl.ANY)
    vmem = pl.BlockSpec(memory_space=pltpu.VMEM)
    dma = pltpu.SemaphoreType.DMA
    rope = jnp.swapaxes(key_rope, 1, 2)[0]
    scaled_out = pl.pallas_call(
        functools.partial(fused_kernel, n, groups),
        out_shape=pltpu.VMEM((tok, width // 2), jnp.bfloat16),
        in_specs=[hbm] * 7,
        out_specs=vmem,
        scratch_shapes=[
            pltpu.VMEM((rows * n, width), jnp.bfloat16),
            pltpu.VMEM((tok * groups, kv_latent.shape[2]), jnp.bfloat16),
            pltpu.VMEM((rope.shape[0], tok * groups), jnp.bfloat16),
            pltpu.VMEM(q_nope.shape[1:], jnp.bfloat16),
            pltpu.VMEM(q_rope.shape[1:], jnp.bfloat16),
            pltpu.VMEM((tok, width // 2), jnp.float32),
            pltpu.VMEM((tok, tok * groups), jnp.float32),
            pltpu.VMEM((tok * groups, width), jnp.float32),
            pltpu.VMEM((2, tok * groups, 2 * DR), jnp.bfloat16),
            pltpu.VMEM((n * groups, 1, LANES), jnp.float32),
            pltpu.SMEM(exponents.shape, jnp.int32),
            pltpu.VMEM(doc_ids.shape, jnp.int32),
            dma((planes, 2, 2)), dma((planes, 2, 2)),
            dma((planes, 2)), dma((planes, 2)), dma((planes, 2)), dma((planes, 2)),
            dma((4, planes, 2)), dma((4, planes, 2)),
            dma((2,)), dma((2,)), dma((6,)), dma, dma, dma,
            pltpu.SemaphoreType.REGULAR, pltpu.SemaphoreType.REGULAR((planes, 2)),
        ],
        compiler_params=pltpu.CompilerParams(collective_id=0, has_side_effects=True),
    )(q_nope[0], q_rope[0], kv_latent[0], rope, weight_codes, exponents, doc_ids)
    return scaled_out[None]


def solution(mesh):
    in_specs = (
        P("fsdp", "ctx", None),
        P("fsdp", "ctx", None),
        P("fsdp", "ctx", None),
        P("fsdp", "ctx", None),
        P("fsdp", None),
        P(),
        P("fsdp", None),
    )
    out_specs = P("fsdp", "ctx", None)
    n, groups = mesh.shape["fsdp"], mesh.shape["ctx"]

    def body(*args):
        rows = args[4].shape[0]
        if groups == 2 and n % 4 == 0 and rows % 32 == 0 and rows * 4 == BLK and n >= 8:
            return fused(n, groups, *args)
        return per_device(*args)

    return jax.shard_map(
        body, mesh=mesh, in_specs=in_specs, out_specs=out_specs, check_vma=False
    )
```

```python
import functools

import jax
import jax.numpy as jnp
from jax import lax
from jax.experimental import pallas as pl
from jax.experimental.pallas import tpu as pltpu
from jax.sharding import PartitionSpec as P

DN = 128
DR = 64
DV = 128
BLK = 128


def dequantize(codes, exponents):
    nrow, ncol = exponents.shape
    factor = jnp.exp2(exponents.astype(jnp.float32)).astype(jnp.bfloat16)
    scaled = codes.reshape(nrow, BLK, ncol, BLK) * factor[:, None, :, None]
    return scaled.reshape(codes.shape)


def attend(queries, rotary, keys_values, rope_all, query_places, query_docs, docs):
    length = keys_values.shape[0]
    k_nope = keys_values[:, :, :DN]
    values = keys_values[:, :, DN:]
    scores = jnp.einsum("qhd,khd->hqk", queries, k_nope, preferred_element_type=jnp.float32)
    scores = scores + jnp.einsum(
        "qhd,kd->hqk", rotary, rope_all, preferred_element_type=jnp.float32
    )
    scores = scores * (DN + DR) ** (-0.5)
    key_places = jnp.arange(length, dtype=jnp.int32)
    allowed = (key_places[None, :] <= query_places[:, None]) & (
        docs[None, :] == query_docs[:, None]
    )
    scores = jnp.where(allowed[None], scores, jnp.float32(-1e30))
    top = jnp.max(scores, axis=-1, keepdims=True)
    expo = jnp.exp(scores - top)
    probs = (expo / jnp.sum(expo, axis=-1, keepdims=True)).astype(jnp.bfloat16)
    return jnp.einsum("hqk,khd->qhd", probs, values, preferred_element_type=jnp.float32)


def per_device(q_nope, q_rope, kv_latent, key_rope, weight_codes, exponents, doc_ids):
    tok = q_nope.shape[1]
    heads = q_nope.shape[2] // DN
    groups = lax.axis_size("ctx")
    length = tok * groups
    offset = lax.axis_index("ctx") * tok
    docs = doc_ids[0]
    latent_all, rope_all = (
        lax.all_gather(kv_latent[0], "ctx", axis=0, tiled=True),
        lax.all_gather(key_rope[0], "ctx", axis=0, tiled=True),
    )
    codes = lax.all_gather(weight_codes, "fsdp", axis=0, tiled=True)
    weight = dequantize(codes, exponents)
    keys_values = jnp.dot(latent_all, weight, preferred_element_type=jnp.float32).astype(
        jnp.bfloat16
    )
    keys_values = keys_values.reshape(length, heads, DN + DV)
    queries = q_nope[0].reshape(tok, heads, DN)
    rotary = q_rope[0].reshape(tok, heads, DR)
    query_docs = lax.dynamic_slice_in_dim(docs, offset, tok)
    query_places = offset + jnp.arange(tok, dtype=jnp.int32)
    attended = attend(queries, rotary, keys_values, rope_all, query_places, query_docs, docs)
    attended = attended.reshape(tok, heads * DV)
    amax = lax.pmax(jnp.max(jnp.abs(attended)), ("fsdp", "ctx"))
    return (attended / amax).reshape(1, tok, heads * DV).astype(jnp.bfloat16)


MESH = pl.DeviceIdType.MESH
LANES = 128
RELAYED = 2


def fused_kernel(
    n, groups, qn_hbm, qr_hbm, lat_hbm, rope_hbm, codes_hbm, expo_hbm, docs_hbm,
    out_ref,
    weight, lat_all, rope_all, qn, qr, attended, bias, partial, rope_of, peaks, expo_ref, docs_ref,
    z_send, z_recv, y_send, y_recv, x_send, x_recv, c_send, c_recv,
    lat_send, lat_recv, local_sem, own_sem, peak_send, peak_recv, ready, entered,
):
    planes = n // 4
    rows, width = codes_hbm.shape
    hr = rows // 2
    tok = qn_hbm.shape[0]
    heads = width // (DN + DV)
    f = lax.axis_index("fsdp")
    x = lax.axis_index("ctx")
    core, row, plane = f % 2, (f // 2) % 2, f // 4

    def at(plane_of, row_of, core_of):
        return (plane_of * 2 + row_of) * 2 + core_of

    def inside(p):
        return (p >= 0) & (p < planes)

    to_core = (at(plane, row, 1 - core), x)
    to_row = (at(plane, 1 - row, core), x)
    to_ctx = (f, 1 - x)
    steps = (1, -1)

    own = pl.ds(pl.multiple_of(x * tok, tok), tok)
    locals_ = [
        pltpu.make_async_copy(lat_hbm, lat_all.at[own], local_sem.at[0]),
        pltpu.make_async_copy(rope_hbm, rope_all.at[:, own], local_sem.at[1]),
        pltpu.make_async_copy(qn_hbm, qn, local_sem.at[2]),
        pltpu.make_async_copy(qr_hbm, qr, local_sem.at[3]),
        pltpu.make_async_copy(expo_hbm, expo_ref, local_sem.at[4]),
        pltpu.make_async_copy(docs_hbm, docs_ref, local_sem.at[5]),
        pltpu.make_async_copy(
            codes_hbm, weight.at[pl.ds(pl.multiple_of(f * rows, rows), rows)], own_sem
        ),
    ]

    barrier = pltpu.get_barrier_semaphore()
    for target in (to_core, to_row, to_ctx):
        pl.semaphore_signal(barrier, inc=1, device_id=target, device_id_type=MESH)
    count = 3
    for step in steps:
        there = inside(plane + step)
        count = count + there.astype(jnp.int32)

        @pl.when(there)
        def _(step=step):
            pl.semaphore_signal(
                barrier, inc=1, device_id=(at(plane + step, row, core), x), device_id_type=MESH
            )

    for copy in locals_:
        copy.start()
    pl.semaphore_wait(barrier, count)

    def piece(plane_of, row_of, core_of, which):
        start = pl.multiple_of(at(plane_of, row_of, core_of) * rows + which * hr, hr)
        return weight.at[pl.ds(start, hr)]

    def own_piece(which):
        return codes_hbm.at[pl.ds(pl.multiple_of(which * hr, hr), hr)]

    def remote(src, dst, send, recv, target):
        return pltpu.make_async_remote_copy(
            src_ref=src, dst_ref=dst, send_sem=send, recv_sem=recv,
            device_id=target, device_id_type=MESH,
        )

    def named(c):
        return x if c == 0 else 1 - x

    def z_out(k, d, c):
        step = steps[d]
        source = plane - step if k == RELAYED else plane
        target = plane + step if k <= RELAYED else plane + step * k
        dst = piece(source, row, core, named(c))
        origin = dst if k == RELAYED else own_piece(named(c))
        copy = remote(
            origin, dst, z_send.at[k, d, c], z_recv.at[k, d, c], (at(target, row, core), x)
        )
        return copy, inside(source) & inside(target)

    def z_in(k, d, c):
        dst = piece(plane - steps[d] * k, row, core, named(c))
        return remote(dst, dst, z_send.at[k, d, c], z_recv.at[k, d, c], to_core)

    def y_out(k, d):
        dst = piece(plane - steps[d] * k, row, core, x)
        origin = dst if k else own_piece(x)
        return remote(origin, dst, y_send.at[k, d], y_recv.at[k, d], to_row)

    def y_in(k, d):
        dst = piece(plane - steps[d] * k, 1 - row, core, x)
        return remote(dst, dst, y_send.at[k, d], y_recv.at[k, d], to_row)

    def x_out(k, d):
        dst = piece(plane - steps[d] * k, 1 - row, core, x)
        return remote(dst, dst, x_send.at[k, d], x_recv.at[k, d], to_ctx)

    def x_in(k, d):
        dst = piece(plane - steps[d] * k, 1 - row, core, 1 - x)
        return remote(dst, dst, x_send.at[k, d], x_recv.at[k, d], to_ctx)

    def core_piece(k, d, which, core_of):
        return piece(
            plane - steps[d] * k, row if which < 2 else 1 - row, core_of, named(which % 2)
        )

    def core_out(k, d, which):
        dst = core_piece(k, d, which, core)
        origin = own_piece(named(which)) if which < 2 and k == 0 else dst
        return remote(origin, dst, c_send.at[which, k, d], c_recv.at[which, k, d], to_core)

    def core_in(k, d, which):
        dst = core_piece(k, d, which, 1 - core)
        return remote(dst, dst, c_send.at[which, k, d], c_recv.at[which, k, d], to_core)

    def each(k, body):
        if k == 0:
            body(0)
        elif k < planes:
            for d, step in enumerate(steps):
                pl.when(inside(plane - step * k))(functools.partial(body, d))

    def z_stage(k, c):
        def body(d):
            z_in(k, d, c).wait_recv()
            if k + 1 == RELAYED:
                onward, there = z_out(RELAYED, d, c)
                pl.when(there)(onward.start)
            if c == 0:
                y_out(k, d).start()
            core_out(k, d, c).start()

        each(k, body)

    def y_stage(k):
        def body(d):
            y_in(k, d).wait_recv()
            x_out(k, d).start()
            core_out(k, d, 2).start()

        each(k, body)

    def x_stage(k):
        def body(d):
            x_in(k, d).wait_recv()
            core_out(k, d, 3).start()

        each(k, body)

    lat_copies = [
        remote(lat_hbm, lat_all.at[own], lat_send.at[0], lat_recv.at[0], to_ctx),
        remote(rope_hbm, rope_all.at[:, own], lat_send.at[1], lat_recv.at[1], to_ctx),
    ]
    from_source = [k for k in range(1, planes) if k != RELAYED]

    def send_own(k, c):
        for d in range(2):
            copy, there = z_out(k, d, c)
            pl.when(there)(copy.start)

    y_out(0, 0).start()
    send_own(1, 0)
    for copy in lat_copies:
        copy.start()
    for c in range(2):
        core_out(0, 0, c).start()
    for r in range(1, planes - 1):
        for d, step in enumerate(steps):

            @pl.when(inside(plane + step) & inside(plane - step * r))
            def _(r=r, d=d, step=step):
                pl.semaphore_signal(
                    entered.at[r, d], inc=1,
                    device_id=(at(plane + step, row, core), x), device_id_type=MESH,
                )

        for d, step in enumerate(steps):

            @pl.when(inside(plane - step * (r + 1)))
            def _(r=r, d=d):
                pl.semaphore_wait(entered.at[r, d], 1)

    for k in from_source[1:]:
        send_own(k, 0)

    z_stage(1, 0)
    y_stage(0)
    send_own(1, 1)
    z_stage(2, 0)
    for k in from_source[1:]:
        send_own(k, 1)
    z_stage(1, 1)
    y_stage(1)
    for k in range(3, planes):
        z_stage(k, 0)
    x_stage(0)

    for copy in locals_:
        copy.wait()
    for copy in lat_copies:
        copy.wait()
    length = lat_all.shape[0]
    docs = docs_ref[...].astype(jnp.float32)
    mine = docs_ref[:, own].astype(jnp.float32)
    mine = jnp.broadcast_to(mine, (tok, tok)).T[:, :1]
    places = lax.broadcasted_iota(jnp.int32, (tok, length), 0) + x * tok
    keys_at = lax.broadcasted_iota(jnp.int32, (tok, length), 1)
    allowed = (keys_at <= places) & (jnp.broadcast_to(docs, (tok, length)) == mine)
    bias[...] = jnp.where(allowed, jnp.float32(0), jnp.float32(-1e30))
    rope = rope_all[...]
    blank = jnp.zeros_like(rope)
    rope_of[0] = jnp.concatenate([rope, blank], axis=0).T
    rope_of[1] = jnp.concatenate([blank, rope], axis=0).T

    wide = DN + DV
    last = jnp.where(plane < planes // 2, planes - 1, 0)

    def product(source, h):
        block = pl.ds(pl.multiple_of(source * BLK, BLK), BLK)
        line = []
        for c in range(wide // BLK):
            power = jnp.full((1, BLK), expo_ref[source, h * wide // BLK + c], jnp.int32)
            factor = jnp.exp2(power.astype(jnp.float32)).astype(jnp.bfloat16)
            line.append(
                weight[block, h * wide + c * BLK : h * wide + (c + 1) * BLK] * factor
            )
        return jnp.dot(
            lat_all[:, block], jnp.concatenate(line, axis=1), preferred_element_type=jnp.float32
        )

    def add_plane(k):
        def body(d):
            source = plane - steps[d] * k
            for which in range(4):
                core_in(k, d, which).wait_recv()

            def add():
                for h in range(heads):
                    columns = slice(h * wide, (h + 1) * wide)
                    if k == 0:
                        partial[:, columns] = product(source, h)
                    else:
                        partial[:, columns] += product(source, h)

            if k == 0:
                add()
            else:
                pl.when(source != last)(add)

        each(k, body)

    y_stage(2)
    add_plane(0)
    for k in range(3, planes):
        y_stage(k)
    x_stage(1)
    for k in range(2, planes):
        z_stage(k, 1)
    x_stage(2)
    add_plane(1)
    for k in range(3, planes):
        x_stage(k)
    for k in range(2, planes):
        add_plane(k)

    pl.semaphore_signal(ready, inc=1, device_id=to_ctx, device_id_type=MESH)

    dims_t = (((1,), (1,)), ((), ()))
    peak = jnp.zeros((tok, DV), jnp.float32)
    for h in range(heads):
        columns = slice(h * wide, (h + 1) * wide)
        kv = (partial[:, columns] + product(last, h)).astype(jnp.bfloat16)
        pair = (h // 2) * 2 * DR
        queries = jnp.concatenate(
            [qn[:, h * DN : (h + 1) * DN], qr[:, pair : pair + 2 * DR]], axis=1
        )
        keys = jnp.concatenate([kv[:, :DN], rope_of[h % 2]], axis=1)
        scores = lax.dot_general(queries, keys, dims_t, preferred_element_type=jnp.float32)
        scores = scores * (DN + DR) ** (-0.5) + bias[...]
        top = jnp.max(scores, axis=-1, keepdims=True)
        expo = jnp.exp(scores - top)
        total = jnp.sum(expo, axis=-1, keepdims=True)
        out = jnp.dot(
            expo.astype(jnp.bfloat16), kv[:, DN:], preferred_element_type=jnp.float32
        ) * (1.0 / total)
        attended[:, h * DV : (h + 1) * DV] = out
        peak = jnp.maximum(peak, jnp.abs(out))

    me = f * groups + x
    peaks[me] = jnp.max(peak, axis=0, keepdims=True)
    pl.semaphore_wait(ready, 1)
    everyone = n * groups

    def peak_to(target):
        remote(peaks.at[me], peaks.at[me], peak_send, peak_recv, target).start()

    for i in range(planes):
        other = lax.rem(2 * planes - 1 - plane - i, planes)
        for pair in range(7, 0, -1):
            ctx_of = x if pair // 4 == 0 else 1 - x
            row_of = row if pair // 2 % 2 == 0 else 1 - row
            core_of = core if pair % 2 == 0 else 1 - core
            peak_to((at(other, row_of, core_of), ctx_of))
        pl.when(other != plane)(functools.partial(peak_to, (at(other, row, core), x)))
    for c in range(2):
        for k in range(1, planes):
            for d in range(2):
                copy, there = z_out(k, d, c)
                pl.when(there)(copy.wait_send)

    def sent(k, d):
        y_out(k, d).wait_send()
        x_out(k, d).wait_send()
        for which in range(4):
            core_out(k, d, which).wait_send()

    for k in range(planes):
        each(k, functools.partial(sent, k))
    others = peaks.at[pl.ds(0, everyone - 1)]
    arrived = remote(others, others, peak_send, peak_recv, to_ctx)
    arrived.wait_send()
    arrived.wait_recv()
    amax = jnp.max(jnp.max(peaks[...], axis=0), axis=-1, keepdims=True)
    out_ref[...] = (attended[...] * (1.0 / amax)).astype(out_ref.dtype)


def fused(n, groups, q_nope, q_rope, kv_latent, key_rope, weight_codes, exponents, doc_ids):
    tok = q_nope.shape[1]
    rows, width = weight_codes.shape
    planes = n // 4
    hbm = pl.BlockSpec(memory_space=pl.ANY)
    vmem = pl.BlockSpec(memory_space=pltpu.VMEM)
    dma = pltpu.SemaphoreType.DMA
    rope = jnp.swapaxes(key_rope, 1, 2)[0]
    scaled_out = pl.pallas_call(
        functools.partial(fused_kernel, n, groups),
        out_shape=pltpu.VMEM((tok, width // 2), jnp.bfloat16),
        in_specs=[hbm] * 7,
        out_specs=vmem,
        scratch_shapes=[
            pltpu.VMEM((rows * n, width), jnp.bfloat16),
            pltpu.VMEM((tok * groups, kv_latent.shape[2]), jnp.bfloat16),
            pltpu.VMEM((rope.shape[0], tok * groups), jnp.bfloat16),
            pltpu.VMEM(q_nope.shape[1:], jnp.bfloat16),
            pltpu.VMEM(q_rope.shape[1:], jnp.bfloat16),
            pltpu.VMEM((tok, width // 2), jnp.float32),
            pltpu.VMEM((tok, tok * groups), jnp.float32),
            pltpu.VMEM((tok * groups, width), jnp.float32),
            pltpu.VMEM((2, tok * groups, 2 * DR), jnp.bfloat16),
            pltpu.VMEM((n * groups, 1, LANES), jnp.float32),
            pltpu.SMEM(exponents.shape, jnp.int32),
            pltpu.VMEM(doc_ids.shape, jnp.int32),
            dma((planes, 2, 2)), dma((planes, 2, 2)),
            dma((planes, 2)), dma((planes, 2)), dma((planes, 2)), dma((planes, 2)),
            dma((4, planes, 2)), dma((4, planes, 2)),
            dma((2,)), dma((2,)), dma((6,)), dma, dma, dma,
            pltpu.SemaphoreType.REGULAR, pltpu.SemaphoreType.REGULAR((planes, 2)),
        ],
        compiler_params=pltpu.CompilerParams(collective_id=0, has_side_effects=True),
    )(q_nope[0], q_rope[0], kv_latent[0], rope, weight_codes, exponents, doc_ids)
    return scaled_out[None]


def solution(mesh):
    in_specs = (
        P("fsdp", "ctx", None),
        P("fsdp", "ctx", None),
        P("fsdp", "ctx", None),
        P("fsdp", "ctx", None),
        P("fsdp", None),
        P(),
        P("fsdp", None),
    )
    out_specs = P("fsdp", "ctx", None)
    n, groups = mesh.shape["fsdp"], mesh.shape["ctx"]

    def body(*args):
        rows = args[4].shape[0]
        if groups == 2 and n % 4 == 0 and rows % 32 == 0 and rows * 4 == BLK and n >= 8:
            return fused(n, groups, *args)
        return per_device(*args)

    return jax.shard_map(
        body, mesh=mesh, in_specs=in_specs, out_specs=out_specs, check_vma=False
    )
```
